128 devices in a mesh: wide: 8 (over z, x_lo), narrow: 16 (over y, x_hi, core).
Axes of the slice: x: 4 (x_hi: 2, x_lo: 2; x = x_hi * 2 + x_lo), y: 4, z: 4, core: 2. Of those that a mesh axis runs over, the one named last changes fastest.
Arguments:
- samples: bfloat16 [1024, 2, 102144], P(('wide', 'narrow')), may hold values from -6 to 6
- filter_taps: float32 [16, 256], replicated, may hold values from -1.5 to 1.5
- beam_weights: bfloat16 [256, 2, 2, 512, 1024], P(('narrow', 'wide')), may hold values from -0.1875 to 0.1875
- smooth_kernel: float32 [33, 33], replicated, may hold values from -0.1875 to 0.1875
Outputs:
- detection: float32 [256, 48, 1024], P('narrow', None, 'wide')
The draws below stay inside these ranges and needn't reach their ends.
All inputs are finite; a program needn't handle non-finite values.
Results may differ from the reference program's by a relative error of at most 0.012.
The reference program's roundings to bfloat16 on the way count: a program that leaves them out, or rounds other values in their place, can miss the bound.
Values may be sent and summed in bfloat16 or wider, within the bound.
No kernel may reach another device: no remote copies, remote signals or barrier semaphores. Data moves between devices by JAX's collectives and lax.ppermute only.
A program may use at most 256 MiB of HBM per device.

```python
import jax
import jax.numpy as jnp
from jax import lax

DISHES = 512
POLS = 2
NFFT = 256
TAPS = 16
BEAMS = 1024
INTEG = 8
HALF = 16
SPECTRA = 384
INPUTS = 1024
CHANNELS = 256
TBINS = 48
SAMPLES = 102144


def levels(stream_key, dims, split, smallest, high):
    def one(axis_at, blocks):
        steps = jax.random.uniform(jax.random.fold_in(jax.random.fold_in(stream_key, 6), axis_at), (blocks,), jnp.float32, smallest / len(split), high / len(split))
        return jnp.repeat(jnp.exp(steps), dims[axis_at] // blocks).reshape((-1,) + (1,) * (len(dims) - axis_at - 1))

    gain = one(*split[0])
    for cut in split[1:]:
        gain = gain * one(*cut)
    return gain


def bell_draw(stream_key, shape, spread, reach, shards=(), kind=jnp.bfloat16):
    array = jax.random.normal(stream_key, shape, jnp.float32) * spread
    if len(shards) > 0:
        array = levels(stream_key, shape, shards, -0.22, 0.18) * array
    return jnp.clip(array, min=-reach, max=reach).astype(kind)


def setup_inputs(seed: int = 0) -> dict:
    arg_keys = jax.random.split(jax.random.key(seed), 5)
    return {
        "samples": bell_draw(arg_keys[0], (INPUTS, 2, SAMPLES), 1.0, 6.0, ((0, 128),)),
        "filter_taps": bell_draw(arg_keys[1], (TAPS, NFFT), TAPS ** -0.5, 1.5, (), jnp.float32),
        "beam_weights": bell_draw(arg_keys[2], (CHANNELS, POLS, 2, DISHES, BEAMS), (2 * DISHES) ** -0.5, 0.1875, ((0, 128),)),
        "smooth_kernel": bell_draw(arg_keys[3], (2 * HALF + 1, 2 * HALF + 1), ((2 * HALF + 1) * (2 * HALF + 1)) ** -0.5, 0.1875, (), jnp.float32),
    }


def fourier_rows(points):
    column = jnp.arange(points, dtype=jnp.int32)
    phase_index = (column[:, None] * column[None, :]) % points
    angles = phase_index.astype(jnp.float32) * jnp.float32(2.0 * jnp.pi / points)
    scale = jnp.float32(1.0 / (points ** 0.5))
    cosine = jnp.cos(angles) * scale
    sine_part = jnp.sin(angles) * scale
    real_row = jnp.stack([cosine, sine_part], axis=1)
    imag_row = jnp.stack([-sine_part, cosine], axis=1)
    return jnp.stack([real_row, imag_row], axis=1).reshape(2 * points, 2, points)


def channelize_one(signal_in, filter_taps, fourier_table):
    tap_count, points = filter_taps.shape
    frames = signal_in.shape[1] // points
    spectra = frames - tap_count + 1
    signal = signal_in.astype(jnp.float32).reshape(2, frames, points)
    windowed = filter_taps[0] * signal[:, 0:spectra]
    for tap_index in range(1, tap_count):
        windowed = windowed + filter_taps[tap_index] * signal[:, tap_index:tap_index + spectra]
    spectrum = jnp.einsum("pab,asb->ps", fourier_table, windowed, precision=lax.Precision.HIGH)
    return spectrum.astype(jnp.bfloat16).reshape(points, 2, spectra)


def channel_power(voltage, weights):
    values = voltage.astype(jnp.float32).reshape(POLS, DISHES, 2, SPECTRA)
    coeffs = weights.astype(jnp.float32)
    real_in = values[:, :, 0]
    imag_in = values[:, :, 1]
    real_w = coeffs[:, 0]
    imag_w = coeffs[:, 1]
    real_out = jnp.einsum("pds,pdb->psb", real_in, real_w) - jnp.einsum("pds,pdb->psb", imag_in, imag_w)
    imag_out = jnp.einsum("pds,pdb->psb", real_in, imag_w) + jnp.einsum("pds,pdb->psb", imag_in, real_w)
    energy = jnp.sum(real_out * real_out + imag_out * imag_out, axis=0)
    binned = energy.reshape(TBINS, INTEG, BEAMS).sum(axis=1)
    return (binned / jnp.float32(POLS * INTEG)).astype(jnp.bfloat16)


def reference(samples, filter_taps, beam_weights, smooth_kernel):
    fourier_table = fourier_rows(NFFT)

    def channelize_input(signal_in):
        return channelize_one(signal_in, filter_taps, fourier_table)

    voltage = lax.map(channelize_input, samples)
    by_channel = jnp.transpose(voltage, (1, 0, 2, 3))

    def power_of(paired):
        return channel_power(paired[0], paired[1])

    intensity = lax.map(power_of, (by_channel, beam_weights))
    values = intensity.astype(jnp.float32)
    centered = values - jnp.mean(values, axis=1, keepdims=True)
    image = jnp.transpose(centered, (2, 0, 1))[:, None]
    kernel = smooth_kernel[None, None]
    filtered = lax.conv_general_dilated(image, kernel, (1, 1), [(HALF, HALF), (HALF, HALF)], precision=lax.Precision.HIGH)
    return jnp.transpose(filtered[:, 0], (1, 2, 0))
```

```python
import functools

import jax
import jax.numpy as jnp
import ml_dtypes
import numpy as np
from jax import lax
from jax.experimental import pallas as pl
from jax.experimental.pallas import tpu as pltpu
from jax.sharding import PartitionSpec as P

INTEG = 8
HALF = 16
LANES = 128
PASSES = 3


def fourier_table(points, wide_count, narrow_count):
    per_device = points // (wide_count * narrow_count)
    slot = np.arange(wide_count * narrow_count)
    first = (slot % narrow_count * wide_count + slot // narrow_count) * per_device
    channel = (first[:, None] + np.arange(per_device)[None, :]).reshape(-1)
    angle = (channel[:, None] * np.arange(points)[None, :] % points) * (2.0 * np.pi / points)
    cosine = np.cos(angle) / np.sqrt(points)
    sine = np.sin(angle) / np.sqrt(points)
    real_row = np.stack([cosine, sine], axis=1)
    imag_row = np.stack([-sine, cosine], axis=1)
    table = np.stack([real_row, imag_row], axis=1)
    halves = points // LANES
    table = table.reshape(points, 2, 2, halves, LANES).transpose(0, 1, 3, 2, 4)
    table = table.reshape(2 * points, 2 * points).astype(np.float32)
    high = table.astype(ml_dtypes.bfloat16)
    low = (table - high.astype(np.float32)).astype(ml_dtypes.bfloat16)
    return high, low


def channelize_kernel(
    frames, spectra, tap_count, group, x_ref, taps_ref, high_ref, low_ref, out_ref, flat, windowed, turned
):
    step = pl.program_id(0)
    bins = spectra // INTEG
    rows = x_ref.shape[0] // group
    per_frame = rows // frames
    flat[...] = x_ref[...].astype(jnp.float32)
    for member in range(group):
        for part in range(per_frame):
            taps = [taps_ref[part // 2, tap] for tap in range(tap_count)]
            for chunk in range(bins // 8):
                totals = [None] * INTEG
                for shift in range(INTEG + tap_count - 1):
                    start = member * rows + per_frame * (shift + chunk * 8 * INTEG) + part
                    values = flat[pl.ds(start, 8, stride=per_frame * INTEG), :]
                    for phase in range(max(0, shift - tap_count + 1), min(INTEG, shift + 1)):
                        term = taps[shift - phase] * values
                        totals[phase] = term if totals[phase] is None else totals[phase] + term
                for phase in range(INTEG):
                    row = member * spectra + phase * bins + chunk * 8
                    windowed[row : row + 8, part * LANES : (part + 1) * LANES] = totals[phase]
    contract = (((1,), (1,)), ((), ()))
    exact = windowed[...]
    high = exact.astype(jnp.bfloat16)
    spectrum = lax.dot_general(high_ref[...], high, contract, preferred_element_type=jnp.float32)
    if PASSES > 1:
        low = (exact - high.astype(jnp.float32)).astype(jnp.bfloat16)
        spectrum += lax.dot_general(high_ref[...], low, contract, preferred_element_type=jnp.float32)
    if PASSES > 2:
        spectrum += lax.dot_general(low_ref[...], high, contract, preferred_element_type=jnp.float32)
    outputs = high_ref.shape[0]
    inputs_here = turned.shape[1] // outputs
    for member in range(group):
        for column in range(spectra // LANES):
            start = member * spectra + column * LANES
            turned[column, pl.ds(step * group + member, outputs, stride=inputs_here), :] = spectrum[
                :, start : start + LANES
            ]

    @pl.when(step == pl.num_programs(0) - 1)
    def _():
        for column in range(spectra // LANES):
            out_ref[:, column * LANES : (column + 1) * LANES] = turned[column].astype(jnp.bfloat16)


def channelize(samples, filter_taps, wide_count, narrow_count):
    inputs_here, _, length = samples.shape
    tap_count, points = filter_taps.shape
    frames = length // points
    spectra = frames - tap_count + 1
    halves = points // LANES
    group = 2
    high, low = fourier_table(points, wide_count, narrow_count)
    lined = samples.reshape(inputs_here, 2, frames, halves, LANES).transpose(0, 2, 3, 1, 4)
    lined = lined.reshape(-1, LANES)
    taps = filter_taps.reshape(tap_count, halves, 1, LANES).transpose(1, 0, 2, 3)
    taps = jnp.broadcast_to(taps, (halves, tap_count, 8, LANES))
    rows = lined.shape[0] // inputs_here * group
    owners = wide_count * narrow_count
    whole = lambda array: pl.BlockSpec(array.shape, lambda i: (0,) * array.ndim)
    voltage = pl.pallas_call(
        functools.partial(channelize_kernel, frames, spectra, tap_count, group),
        out_shape=jax.ShapeDtypeStruct((2 * points * inputs_here, spectra), jnp.bfloat16),
        grid=(inputs_here // group,),
        in_specs=[
            pl.BlockSpec((rows, LANES), lambda i: (i, 0)),
            whole(taps),
            whole(high),
            whole(low),
        ],
        out_specs=pl.BlockSpec((2 * points * inputs_here, spectra), lambda i: (0, 0)),
        scratch_shapes=[
            pltpu.VMEM((rows, LANES), jnp.float32),
            pltpu.VMEM((group * spectra, 2 * points), jnp.float32),
            pltpu.VMEM((spectra // LANES, 2 * points * inputs_here, LANES), jnp.float32),
        ],
        compiler_params=pltpu.CompilerParams(vmem_limit_bytes=40 << 20),
        name="channelize",
    )(lined, taps, jnp.asarray(high), jnp.asarray(low))
    return voltage.reshape(owners, points // owners, 2, inputs_here, spectra)


def beam_kernel(scale, volt_ref, weight_ref, out_ref, total):
    pol = pl.program_id(1)
    sources, _, _, inputs, spectra = volt_ref.shape
    dishes = sources * inputs
    bins = spectra // INTEG
    real = volt_ref[:, 0, 0].reshape(dishes, spectra).T
    imag = volt_ref[:, 0, 1].reshape(dishes, spectra).T
    lhs = jnp.concatenate(
        [jnp.concatenate([real, -imag], axis=1), jnp.concatenate([imag, real], axis=1)], axis=0
    )
    beams = weight_ref.shape[-1]
    width = 256
    for block in range(beams // width):
        columns = slice(block * width, (block + 1) * width)
        weights = weight_ref[0, 0, :, :, columns].reshape(2 * dishes, width)
        formed = jnp.dot(lhs, weights, preferred_element_type=jnp.float32)
        power = formed * formed
        power = power[:spectra] + power[spectra:]
        binned = power[0:bins]
        for phase in range(1, INTEG):
            binned = binned + power[phase * bins : (phase + 1) * bins]

        @pl.when(pol == 0)
        def _():
            total[:, columns] = binned

        @pl.when(pol > 0)
        def _():
            total[:, columns] += binned

    @pl.when(pol == pl.num_programs(1) - 1)
    def _():
        chunk = out_ref.shape[-1]
        for owner in range(out_ref.shape[0]):
            values = total[:, owner * chunk : (owner + 1) * chunk] * jnp.float32(scale)
            out_ref[owner, 0] = values.astype(jnp.bfloat16)


def beam_power(turned, beam_weights, wide_count):
    sources, per_device, _, inputs, spectra = turned.shape
    pols, dishes, beams = beam_weights.shape[1], beam_weights.shape[3], beam_weights.shape[4]
    bins = spectra // INTEG
    return pl.pallas_call(
        functools.partial(beam_kernel, 1.0 / (pols * INTEG)),
        out_shape=jax.ShapeDtypeStruct((wide_count, per_device, bins, beams // wide_count), jnp.bfloat16),
        grid=(per_device, pols),
        in_specs=[
            pl.BlockSpec((sources // pols, 1, 2, inputs, spectra), lambda c, p: (p, c, 0, 0, 0)),
            pl.BlockSpec((1, 1, 2, dishes, beams), lambda c, p: (c, p, 0, 0, 0)),
        ],
        out_specs=pl.BlockSpec((wide_count, 1, bins, beams // wide_count), lambda c, p: (0, c, 0, 0)),
        scratch_shapes=[pltpu.VMEM((bins, beams), jnp.float32)],
        compiler_params=pltpu.CompilerParams(vmem_limit_bytes=40 << 20),
        name="beam_power",
    )(turned, beam_weights)


def banded(smooth_kernel, channels_here, bins):
    extent = smooth_kernel.shape[0]
    half = extent // 2
    positions = jnp.arange(bins, dtype=jnp.int32)
    distance = positions[None, :] - positions[:, None] + half
    selector = (distance[None] == jnp.arange(extent, dtype=jnp.int32)[:, None, None]).astype(jnp.bfloat16)
    toeplitz = jnp.einsum(
        "dtu,kd->tku", selector, smooth_kernel.astype(jnp.bfloat16), preferred_element_type=jnp.float32
    ).astype(jnp.bfloat16)
    row = toeplitz.reshape(bins, extent * bins)
    shifted = [
        jnp.pad(row, ((0, 0), (c * bins, (channels_here - 1 - c) * bins))) for c in range(channels_here)
    ]
    return jnp.concatenate(shifted, axis=0)


def smooth_body(low_ref, mid_ref, high_ref, matrix_ref, out_ref):
    channels, bins, beams = mid_ref.shape
    centered = []
    for ref in (low_ref, mid_ref, high_ref):
        values = ref[...].astype(jnp.float32)
        values = values - jnp.mean(values, axis=1, keepdims=True)
        centered.append(values.astype(jnp.bfloat16).reshape(channels * bins, beams))
    stacked = jnp.concatenate(centered, axis=0)
    result = jnp.dot(matrix_ref[...], stacked, preferred_element_type=jnp.float32)
    out_ref[...] = result.reshape(channels, bins, beams)


def smooth(low, mid, high, matrix):
    vmem = pl.BlockSpec(memory_space=pltpu.VMEM)
    return pl.pallas_call(
        smooth_body,
        out_shape=jax.ShapeDtypeStruct(mid.shape, jnp.float32),
        in_specs=[vmem] * 4,
        out_specs=vmem,
        compiler_params=pltpu.CompilerParams(vmem_limit_bytes=40 << 20),
        name="smooth",
    )(low, mid, high, matrix)


def body(samples, filter_taps, beam_weights, smooth_kernel):
    wide_count = lax.axis_size("wide")
    narrow_count = lax.axis_size("narrow")
    voltage = channelize(samples, filter_taps, wide_count, narrow_count)
    voltage, smooth_kernel = lax.optimization_barrier((voltage, smooth_kernel))
    turned = lax.all_to_all(voltage, ("wide", "narrow"), split_axis=0, concat_axis=0, tiled=True)
    intensity = beam_power(turned, beam_weights, wide_count)
    bins, beams = intensity.shape[2], intensity.shape[3]
    by_beam = lax.all_to_all(intensity, "wide", split_axis=0, concat_axis=0, tiled=True)
    by_beam = by_beam.reshape(-1, bins, beams)
    forward = [(i, i + 1) for i in range(narrow_count - 1)]
    backward = [(target, source) for source, target in forward]
    low = lax.ppermute(by_beam, "narrow", forward)
    high = lax.ppermute(by_beam, "narrow", backward)
    return smooth(low, by_beam, high, banded(smooth_kernel, by_beam.shape[0], bins))


def solution(mesh):
    placed = (
        P(("wide", "narrow"), None, None),
        P(),
        P(("narrow", "wide"), None, None, None, None),
        P(),
    )
    return jax.shard_map(
        body, mesh=mesh, in_specs=placed, out_specs=P("narrow", None, "wide"), check_vma=False
    )
```

```python
import functools

import jax
import jax.numpy as jnp
import ml_dtypes
import numpy as np
from jax import lax
from jax.experimental import pallas as pl
from jax.experimental.pallas import tpu as pltpu
from jax.sharding import PartitionSpec as P

INTEG = 8
HALF = 16
LANES = 128


def fourier_table(points, wide_count, narrow_count):
    per_device = points // (wide_count * narrow_count)
    slot = np.arange(wide_count * narrow_count)
    first = (slot % narrow_count * wide_count + slot // narrow_count) * per_device
    channel = (first[:, None] + np.arange(per_device)[None, :]).reshape(-1)
    angle = (channel[:, None] * np.arange(points)[None, :] % points) * (2.0 * np.pi / points)
    cosine = np.cos(angle) / np.sqrt(points)
    sine = np.sin(angle) / np.sqrt(points)
    real_row = np.stack([cosine, sine], axis=1)
    imag_row = np.stack([-sine, cosine], axis=1)
    table = np.stack([real_row, imag_row], axis=1)
    halves = points // LANES
    table = table.reshape(points, 2, 2, halves, LANES).transpose(0, 1, 3, 2, 4)
    table = table.reshape(2 * points, 2 * points).astype(np.float32)
    high = table.astype(ml_dtypes.bfloat16)
    low = (table - high.astype(np.float32)).astype(ml_dtypes.bfloat16)
    return high, low


def channelize_kernel(
    frames, spectra, tap_count, group, x_ref, taps_ref, high_ref, out_ref, lined, windowed, turned
):
    step = pl.program_id(0)
    rows = x_ref.shape[0] // group
    per_frame = rows // frames
    segment = spectra // 8
    span = segment * per_frame
    needed = (segment + tap_count - 1) * per_frame
    pitch = lined.shape[0] // group
    half_taps = tap_count // 2
    pairs = segment // 2

    for member in range(group):
        for lane in range(8):
            count = min(-(-needed // 8) * 8, rows - lane * span)
            start = member * rows + lane * span
            values = x_ref[start : start + count, :].astype(jnp.float32)
            lined[pl.ds(member * pitch + lane, count, stride=8), :] = values

    def window(member, part):
        half = part // 2
        columns = slice(half * LANES, (half + 1) * LANES)
        taps = [jnp.broadcast_to(taps_ref[t : t + 1, columns], (8, LANES)) for t in range(tap_count)]
        even, odd = taps[0::2], taps[1::2]
        both = [first + second for first, second in zip(even, odd)]

        def frame(index):
            start = member * pitch + (per_frame * index + part) * 8
            return lined[start : start + 8, :]

        def put(index, values):
            row = member * spectra + index * 8
            windowed[row : row + 8, part * LANES : (part + 1) * LANES] = values

        def feed(totals, factors, values, index, count):
            for tap in range(half_taps):
                target = index - tap
                if 0 <= target < count:
                    term = factors[tap] * values
                    totals[target] = totals[target] + term if target in totals else term

        evens, odds, sums = {}, {}, {}
        late = None
        for index in range(pairs + half_taps):
            early = frame(2 * index)
            feed(evens, even, early, index, pairs + 1)
            if index > 0:
                feed(odds, odd, late, index - 1, pairs)
                feed(sums, both, late + early, index - 1, pairs)
                done = index - half_taps
                if done >= 0:
                    second = odds.pop(done)
                    put(2 * done, evens[done] + second)
                    put(2 * done + 1, sums.pop(done) - (evens[done + 1] + second))
                    evens.pop(done)
            if index < pairs + half_taps - 1:
                late = frame(2 * index + 1)

    contract = (((1,), (1,)), ((), ()))
    outputs = high_ref.shape[0]
    inputs_here = turned.shape[1] // outputs
    for member in range(group):
        for part in range(per_frame):
            window(member, part)
        high = windowed[member * spectra : (member + 1) * spectra, :].astype(jnp.bfloat16)
        spectrum = lax.dot_general(high_ref[...], high, contract, preferred_element_type=jnp.float32)
        for column in range(spectra // LANES):
            turned[column, pl.ds(step * group + member, outputs, stride=inputs_here), :] = spectrum[
                :, column * LANES : (column + 1) * LANES
            ]

    @pl.when(step == pl.num_programs(0) - 1)
    def _():
        for column in range(spectra // LANES):
            out_ref[:, column * LANES : (column + 1) * LANES] = turned[column].astype(jnp.bfloat16)


def channelize(samples, filter_taps, wide_count, narrow_count):
    inputs_here, _, length = samples.shape
    tap_count, points = filter_taps.shape
    frames = length // points
    spectra = frames - tap_count + 1
    halves = points // LANES
    group = 4
    high, _ = fourier_table(points, wide_count, narrow_count)
    lined = samples.reshape(inputs_here, 2, frames, halves, LANES).transpose(0, 2, 3, 1, 4)
    lined = lined.reshape(-1, LANES)
    rows = lined.shape[0] // inputs_here * group
    owners = wide_count * narrow_count
    pitch = -(-(spectra // 8 + tap_count - 1) * 2 * halves // 8) * 64
    whole = lambda array: pl.BlockSpec(array.shape, lambda i: (0,) * array.ndim)
    voltage = pl.pallas_call(
        functools.partial(channelize_kernel, frames, spectra, tap_count, group),
        out_shape=jax.ShapeDtypeStruct((2 * points * inputs_here, spectra), jnp.bfloat16),
        grid=(inputs_here // group,),
        in_specs=[
            pl.BlockSpec((rows, LANES), lambda i: (i, 0)),
            whole(filter_taps),
            whole(high),
        ],
        out_specs=pl.BlockSpec((2 * points * inputs_here, spectra), lambda i: (0, 0)),
        scratch_shapes=[
            pltpu.VMEM((group * pitch, LANES), jnp.float32),
            pltpu.VMEM((group * spectra, 2 * points), jnp.float32),
            pltpu.VMEM((spectra // LANES, 2 * points * inputs_here, LANES), jnp.float32),
        ],
        compiler_params=pltpu.CompilerParams(vmem_limit_bytes=60 << 20),
        name="channelize",
    )(lined, filter_taps, jnp.asarray(high))
    return voltage.reshape(owners, points // owners, 2, inputs_here, spectra)


def beam_kernel(scale, volt_ref, weight_ref, out_ref, held, arrived):
    sources, per_device, _, inputs, spectra = volt_ref.shape
    pols, beams = weight_ref.shape[1], weight_ref.shape[-1]
    each = sources // pols
    dishes = each * inputs
    owners, chunk = out_ref.shape[0], out_ref.shape[-1]
    copies = {}
    for channel in range(per_device):
        for pol in range(pols):
            copies[channel, pol] = pltpu.make_async_copy(
                weight_ref.at[channel, pol], held.at[channel, pol], arrived.at[channel, pol]
            )
            copies[channel, pol].start()
    for channel in range(per_device):
        total = None
        for pol in range(pols):
            rows = slice(pol * each, (pol + 1) * each)
            real = volt_ref[rows, channel, 0].reshape(dishes, spectra).T
            imag = volt_ref[rows, channel, 1].reshape(dishes, spectra).T
            lhs = jnp.concatenate(
                [jnp.concatenate([real, -imag], axis=1), jnp.concatenate([imag, real], axis=1)], axis=0
            )
            copies[channel, pol].wait()
            weights = held[channel, pol].reshape(2 * dishes, beams)
            formed = jnp.dot(lhs, weights, preferred_element_type=jnp.float32)
            power = formed * formed
            power = power[:spectra] + power[spectra:]
            power = power.reshape(spectra // (8 * INTEG), INTEG, 8, beams).sum(axis=1)
            total = power if total is None else total + power
        total = (total.reshape(spectra // INTEG, beams) * jnp.float32(scale)).astype(jnp.bfloat16)
        for owner in range(owners):
            out_ref[owner, channel] = total[:, owner * chunk : (owner + 1) * chunk]


def beam_power(turned, weights, wide_count):
    per_device, spectra = turned.shape[1], turned.shape[4]
    pols, beams = weights.shape[1], weights.shape[4]
    bins = spectra // INTEG
    vmem = pl.BlockSpec(memory_space=pltpu.VMEM)
    return pl.pallas_call(
        functools.partial(beam_kernel, 1.0 / (pols * INTEG)),
        out_shape=jax.ShapeDtypeStruct((wide_count, per_device, bins, beams // wide_count), jnp.bfloat16),
        in_specs=[vmem, pl.BlockSpec(memory_space=pl.ANY)],
        out_specs=vmem,
        scratch_shapes=[
            pltpu.VMEM(weights.shape, weights.dtype),
            pltpu.SemaphoreType.DMA((per_device, pols)),
        ],
        compiler_params=pltpu.CompilerParams(vmem_limit_bytes=50 << 20),
        name="beam_power",
    )(turned, weights)


def band_kernel(row_ref, out_ref):
    bins, width = row_ref.shape
    for channel in range(out_ref.shape[0] // bins):
        shifted = pltpu.roll(row_ref[...], channel * bins, axis=1)
        out_ref[channel * bins : (channel + 1) * bins, :] = shifted.astype(jnp.bfloat16)


def banded(smooth_kernel, channels_here, bins):
    extent = smooth_kernel.shape[0]
    half = extent // 2
    stored = np.arange(bins) // 8 + np.arange(bins) % 8 * (bins // 8)
    distance = stored[None, :] - np.arange(bins)[:, None] + half
    selector = (distance[None] == np.arange(extent)[:, None, None]).astype(ml_dtypes.bfloat16)
    row = jnp.einsum(
        "dtu,kd->tku",
        jnp.asarray(selector),
        smooth_kernel.astype(jnp.bfloat16),
        preferred_element_type=jnp.float32,
    ).reshape(bins, extent * bins)
    width = (channels_here + extent - 1) * bins
    row = jnp.pad(row, ((0, 0), (0, width - extent * bins)))
    vmem = pl.BlockSpec(memory_space=pltpu.VMEM)
    return pl.pallas_call(
        band_kernel,
        out_shape=jax.ShapeDtypeStruct((channels_here * bins, width), jnp.bfloat16),
        in_specs=[vmem],
        out_specs=vmem,
        compiler_params=pltpu.CompilerParams(vmem_limit_bytes=16 << 20),
        name="band",
    )(row)


def smooth_body(low_ref, mid_ref, high_ref, matrix_ref, out_ref):
    channels, bins, beams = mid_ref.shape
    centered = []
    for ref in (low_ref, mid_ref, high_ref):
        values = ref[...].astype(jnp.float32)
        values = values - jnp.mean(values, axis=1, keepdims=True)
        centered.append(values.astype(jnp.bfloat16).reshape(channels * bins, beams))
    stacked = jnp.concatenate(centered, axis=0)
    result = jnp.dot(matrix_ref[...], stacked, preferred_element_type=jnp.float32)
    out_ref[...] = result.reshape(channels, bins, beams)


def smooth(low, mid, high, matrix):
    vmem = pl.BlockSpec(memory_space=pltpu.VMEM)
    return pl.pallas_call(
        smooth_body,
        out_shape=jax.ShapeDtypeStruct(mid.shape, jnp.float32),
        in_specs=[vmem] * 4,
        out_specs=vmem,
        compiler_params=pltpu.CompilerParams(vmem_limit_bytes=16 << 20),
        name="smooth",
    )(low, mid, high, matrix)


def body(samples, filter_taps, beam_weights, smooth_kernel):
    wide_count = lax.axis_size("wide")
    narrow_count = lax.axis_size("narrow")
    voltage = channelize(samples, filter_taps, wide_count, narrow_count)
    voltage, smooth_kernel = lax.optimization_barrier((voltage, smooth_kernel))
    turned = lax.all_to_all(voltage, ("wide", "narrow"), split_axis=0, concat_axis=0, tiled=True)
    per_device, spectra = turned.shape[1], turned.shape[4]
    matrix = banded(smooth_kernel, per_device * wide_count, spectra // INTEG)
    turned, matrix = lax.optimization_barrier((turned, matrix))
    intensity = beam_power(turned, beam_weights, wide_count)
    bins, beams = intensity.shape[2], intensity.shape[3]
    by_beam = lax.all_to_all(intensity, "wide", split_axis=0, concat_axis=0, tiled=True)
    by_beam = by_beam.reshape(-1, bins, beams)
    forward = [(i, i + 1) for i in range(narrow_count - 1)]
    backward = [(target, source) for source, target in forward]
    low = lax.ppermute(by_beam, "narrow", forward)
    high = lax.ppermute(by_beam, "narrow", backward)
    return smooth(low, by_beam, high, matrix)


def solution(mesh):
    placed = (
        P(("wide", "narrow"), None, None),
        P(),
        P(("narrow", "wide"), None, None, None, None),
        P(),
    )
    return jax.shard_map(
        body, mesh=mesh, in_specs=placed, out_specs=P("narrow", None, "wide"), check_vma=False
    )
```

```python
import functools

import jax
import jax.numpy as jnp
import ml_dtypes
import numpy as np
from jax import lax
from jax.experimental import pallas as pl
from jax.experimental.pallas import tpu as pltpu
from jax.sharding import PartitionSpec as P

INTEG = 8
HALF = 16
LANES = 128
BATCH = 2


def fourier_table(points, wide_count, narrow_count):
    per_device = points // (wide_count * narrow_count)
    slot = np.arange(wide_count * narrow_count)
    first = (slot % narrow_count * wide_count + slot // narrow_count) * per_device
    channel = first[None, :] + np.arange(per_device)[:, None]
    angle = (channel[:, :, None] * np.arange(points // 2) % points) * (2.0 * np.pi / points)
    cosine = np.cos(angle) / np.sqrt(points)
    sine = np.sin(angle) / np.sqrt(points)
    real_row = np.concatenate([cosine, sine], axis=2)
    imag_row = np.concatenate([-sine, cosine], axis=2)
    table = np.stack([real_row, imag_row], axis=2).reshape(per_device, -1, points)
    table = table.astype(np.float32)
    high = table.astype(ml_dtypes.bfloat16)
    low = (table - high.astype(np.float32)).astype(ml_dtypes.bfloat16)
    return np.concatenate([high, high, low], axis=2)


def channelize_kernel(
    frames, spectra, tap_count, group, x_ref, taps_ref, table_ref, out_ref, lined, windowed, turned
):
    step = pl.program_id(0)
    rows = x_ref.shape[0] // group
    per_frame = rows // frames
    segment = spectra // 8
    span = segment * per_frame
    needed = (segment + tap_count - 1) * per_frame
    pitch = lined.shape[0] // group
    half_taps = tap_count // 2
    pairs = segment // 2

    for member in range(group):
        for lane in range(8):
            count = min(-(-needed // 8) * 8, rows - lane * span)
            start = member * rows + lane * span
            values = x_ref[start : start + count, :].astype(jnp.float32)
            lined[pl.ds(member * pitch + lane, count, stride=8), :] = values

    def window(member, part):
        half = part // 2
        columns = slice(half * LANES, (half + 1) * LANES)
        taps = [jnp.broadcast_to(taps_ref[t : t + 1, columns], (8, LANES)) for t in range(tap_count)]
        even, odd = taps[0::2], taps[1::2]
        both = [first + second for first, second in zip(even, odd)]

        def frame(index):
            start = member * pitch + (per_frame * index + part) * 8
            return lined[start : start + 8, :]

        def put(index, values):
            row = member * spectra + index * 8
            windowed[row : row + 8, part * LANES : (part + 1) * LANES] = values

        def feed(totals, factors, values, index, count):
            for tap in range(half_taps):
                target = index - tap
                if 0 <= target < count:
                    term = factors[tap] * values
                    totals[target] = totals[target] + term if target in totals else term

        evens, odds, sums = {}, {}, {}
        late = None
        for index in range(pairs + half_taps):
            early = frame(2 * index)
            feed(evens, even, early, index, pairs + 1)
            if index > 0:
                feed(odds, odd, late, index - 1, pairs)
                feed(sums, both, late + early, index - 1, pairs)
                done = index - half_taps
                if done >= 0:
                    second = odds.pop(done)
                    put(2 * done, evens[done] + second)
                    put(2 * done + 1, sums.pop(done) - (evens[done + 1] + second))
                    evens.pop(done)
            if index < pairs + half_taps - 1:
                late = frame(2 * index + 1)

    contract = (((1,), (1,)), ((), ()))
    parities, outputs, points = table_ref.shape[0], table_ref.shape[1], windowed.shape[1]
    inputs_here = turned.shape[1] // (parities * outputs)
    batch = BATCH
    for first in range(0, group, batch):
        for member in range(first, first + batch):
            for part in range(per_frame):
                window(member, part)
        rows = slice(first * spectra, (first + batch) * spectra)
        near = windowed[rows, : points // 2]
        far = windowed[rows, points // 2 :]
        for parity in range(parities):
            folded = near + far if parity == 0 else near - far
            high = folded.astype(jnp.bfloat16)
            low = (folded - high.astype(jnp.float32)).astype(jnp.bfloat16)
            spectrum = lax.dot_general(
                table_ref[parity],
                jnp.concatenate([high, low, high], axis=1),
                contract,
                preferred_element_type=jnp.float32,
            )
            for member in range(batch):
                start = parity * outputs * inputs_here + step * group + first + member
                for column in range(spectra // LANES):
                    left = member * spectra + column * LANES
                    turned[column, pl.ds(start, outputs, stride=inputs_here), :] = spectrum[
                        :, left : left + LANES
                    ]

    @pl.when(step == pl.num_programs(0) - 1)
    def _():
        for column in range(spectra // LANES):
            columns = slice(column * LANES, (column + 1) * LANES)
            for parity in range(parities):
                count = outputs * inputs_here
                values = turned[column, parity * count : (parity + 1) * count, :].astype(jnp.bfloat16)
                out_ref[:, parity, :, columns] = values.reshape(out_ref.shape[0], -1, LANES)


def channelize(samples, filter_taps, wide_count, narrow_count):
    inputs_here, _, length = samples.shape
    tap_count, points = filter_taps.shape
    frames = length // points
    spectra = frames - tap_count + 1
    halves = points // LANES
    group = 4
    table = fourier_table(points, wide_count, narrow_count)
    lined = samples.reshape(inputs_here, 2, frames, halves, LANES).transpose(0, 2, 3, 1, 4)
    lined = lined.reshape(-1, LANES)
    rows = lined.shape[0] // inputs_here * group
    owners = wide_count * narrow_count
    shape = (owners, points // owners, 2 * inputs_here, spectra)
    pitch = -(-(spectra // 8 + tap_count - 1) * 2 * halves // 8) * 64
    whole = lambda array: pl.BlockSpec(array.shape, lambda i: (0,) * array.ndim)
    voltage = pl.pallas_call(
        functools.partial(channelize_kernel, frames, spectra, tap_count, group),
        out_shape=jax.ShapeDtypeStruct(shape, jnp.bfloat16),
        grid=(inputs_here // group,),
        in_specs=[
            pl.BlockSpec((rows, LANES), lambda i: (i, 0)),
            whole(filter_taps),
            whole(table),
        ],
        out_specs=pl.BlockSpec(shape, lambda i: (0, 0, 0, 0)),
        scratch_shapes=[
            pltpu.VMEM((group * pitch, LANES), jnp.float32),
            pltpu.VMEM((group * spectra, 2 * points), jnp.float32),
            pltpu.VMEM((spectra // LANES, 2 * points * inputs_here, LANES), jnp.float32),
        ],
        compiler_params=pltpu.CompilerParams(vmem_limit_bytes=60 << 20),
        name="channelize",
    )(lined, filter_taps, jnp.asarray(table))
    return voltage.reshape(owners, points // owners, 2, inputs_here, spectra)


def beam_kernel(scale, volt_ref, weight_ref, out_ref, held, arrived):
    sources, per_device, _, inputs, spectra = volt_ref.shape
    pols, beams = weight_ref.shape[1], weight_ref.shape[-1]
    each = sources // pols
    dishes = each * inputs
    owners, chunk = out_ref.shape[0], out_ref.shape[-1]
    copies = {}
    for channel in range(per_device):
        for pol in range(pols):
            copies[channel, pol] = pltpu.make_async_copy(
                weight_ref.at[channel, pol], held.at[channel, pol], arrived.at[channel, pol]
            )
            copies[channel, pol].start()
    for channel in range(per_device):
        total = None
        for pol in range(pols):
            rows = slice(pol * each, (pol + 1) * each)
            real = volt_ref[rows, channel, 0].reshape(dishes, spectra).T
            imag = volt_ref[rows, channel, 1].reshape(dishes, spectra).T
            lhs = jnp.concatenate(
                [jnp.concatenate([real, -imag], axis=1), jnp.concatenate([imag, real], axis=1)], axis=0
            )
            copies[channel, pol].wait()
            weights = held[channel, pol].reshape(2 * dishes, beams)
            formed = jnp.dot(lhs, weights, preferred_element_type=jnp.float32)
            power = formed * formed
            power = power[:spectra] + power[spectra:]
            power = power.reshape(spectra // (8 * INTEG), INTEG, 8, beams).sum(axis=1)
            total = power if total is None else total + power
        total = (total.reshape(spectra // INTEG, beams) * jnp.float32(scale)).astype(jnp.bfloat16)
        for owner in range(owners):
            out_ref[owner, channel] = total[:, owner * chunk : (owner + 1) * chunk]


def beam_power(turned, weights, wide_count):
    per_device, spectra = turned.shape[1], turned.shape[4]
    pols, beams = weights.shape[1], weights.shape[4]
    bins = spectra // INTEG
    vmem = pl.BlockSpec(memory_space=pltpu.VMEM)
    return pl.pallas_call(
        functools.partial(beam_kernel, 1.0 / (pols * INTEG)),
        out_shape=jax.ShapeDtypeStruct((wide_count, per_device, bins, beams // wide_count), jnp.bfloat16),
        in_specs=[vmem, pl.BlockSpec(memory_space=pl.ANY)],
        out_specs=vmem,
        scratch_shapes=[
            pltpu.VMEM(weights.shape, weights.dtype),
            pltpu.SemaphoreType.DMA((per_device, pols)),
        ],
        compiler_params=pltpu.CompilerParams(vmem_limit_bytes=50 << 20),
        name="beam_power",
    )(turned, weights)


def band_kernel(odd_ref, row_ref, out_ref):
    bins, width = row_ref.shape
    block = out_ref.shape[0]
    odd = odd_ref[0] > 0
    for channel in range(block // bins):
        rows = slice(channel * bins, (channel + 1) * bins)
        shifted = pltpu.roll(row_ref[...], channel * bins, axis=1)
        low, high = shifted[:, :block], shifted[:, width - block :]
        out_ref[rows, :block] = jnp.where(odd, low, high).astype(jnp.bfloat16)
        out_ref[rows, block : width - block] = shifted[:, block : width - block].astype(jnp.bfloat16)
        out_ref[rows, width - block :] = jnp.where(odd, high, low).astype(jnp.bfloat16)


def banded(smooth_kernel, odd, channels_here, bins):
    extent = smooth_kernel.shape[0]
    half = extent // 2
    stored = np.arange(bins) // 8 + np.arange(bins) % 8 * (bins // 8)
    distance = stored[None, :] - np.arange(bins)[:, None] + half
    selector = (distance[None] == np.arange(extent)[:, None, None]).astype(ml_dtypes.bfloat16)
    row = jnp.einsum(
        "dtu,kd->tku",
        jnp.asarray(selector),
        smooth_kernel.astype(jnp.bfloat16),
        preferred_element_type=jnp.float32,
    ).reshape(bins, extent * bins)
    width = (channels_here + extent - 1) * bins
    row = jnp.pad(row, ((0, 0), (0, width - extent * bins)))
    vmem = pl.BlockSpec(memory_space=pltpu.VMEM)
    return pl.pallas_call(
        band_kernel,
        out_shape=jax.ShapeDtypeStruct((channels_here * bins, width), jnp.bfloat16),
        in_specs=[pl.BlockSpec(memory_space=pltpu.SMEM), vmem],
        out_specs=vmem,
        compiler_params=pltpu.CompilerParams(vmem_limit_bytes=16 << 20),
        name="band",
    )(odd.astype(jnp.int32).reshape(1), row)


def smooth_body(pair_ref, mid_ref, next_ref, matrix_ref, out_ref):
    channels, bins, beams = mid_ref.shape
    centered = []
    for ref in (pair_ref, mid_ref, next_ref):
        values = ref[...].astype(jnp.float32)
        values = values - jnp.mean(values, axis=1, keepdims=True)
        centered.append(values.astype(jnp.bfloat16).reshape(channels * bins, beams))
    stacked = jnp.concatenate(centered, axis=0)
    result = jnp.dot(matrix_ref[...], stacked, preferred_element_type=jnp.float32)
    out_ref[...] = result.reshape(channels, bins, beams)


def smooth(pair, mid, other, matrix):
    vmem = pl.BlockSpec(memory_space=pltpu.VMEM)
    return pl.pallas_call(
        smooth_body,
        out_shape=jax.ShapeDtypeStruct(mid.shape, jnp.float32),
        in_specs=[vmem] * 4,
        out_specs=vmem,
        compiler_params=pltpu.CompilerParams(vmem_limit_bytes=16 << 20),
        name="smooth",
    )(pair, mid, other, matrix)


def body(samples, filter_taps, beam_weights, smooth_kernel):
    wide_count = lax.axis_size("wide")
    narrow_count = lax.axis_size("narrow")
    voltage = channelize(samples, filter_taps, wide_count, narrow_count)
    voltage, smooth_kernel = lax.optimization_barrier((voltage, smooth_kernel))
    turned = lax.all_to_all(voltage, ("wide", "narrow"), split_axis=0, concat_axis=0, tiled=True)
    per_device, spectra = turned.shape[1], turned.shape[4]
    odd = lax.axis_index("narrow") % 2
    matrix = banded(smooth_kernel, odd, per_device * wide_count, spectra // INTEG)
    turned, matrix = lax.optimization_barrier((turned, matrix))
    intensity = beam_power(turned, beam_weights, wide_count)
    bins, beams = intensity.shape[2], intensity.shape[3]
    by_beam = lax.all_to_all(intensity, "wide", split_axis=0, concat_axis=0, tiled=True)
    by_beam = by_beam.reshape(-1, bins, beams)
    pairs = [(i, i ^ 1) for i in range(narrow_count)]
    others = [(i, i - 1 + i % 2 * 2) for i in range(1, narrow_count - 1)]
    other = lax.ppermute(by_beam, "narrow", others)
    pair = lax.ppermute(by_beam, "narrow", pairs)
    return smooth(pair, by_beam, other, matrix)


def solution(mesh):
    placed = (
        P(("wide", "narrow"), None, None),
        P(),
        P(("narrow", "wide"), None, None, None, None),
        P(),
    )
    return jax.shard_map(
        body, mesh=mesh, in_specs=placed, out_specs=P("narrow", None, "wide"), check_vma=False
    )
```

```python
import functools

import jax
import jax.numpy as jnp
import ml_dtypes
import numpy as np
from jax import lax
from jax.experimental import pallas as pl
from jax.experimental.pallas import tpu as pltpu
from jax.sharding import PartitionSpec as P

INTEG = 8
HALF = 16
LANES = 128
BATCH = 2


def fourier_table(points, owners):
    per_device = points // owners
    first = np.arange(owners) * per_device
    channel = first[None, :] + np.arange(per_device)[:, None]
    angle = (channel[:, :, None] * np.arange(points // 2) % points) * (2.0 * np.pi / points)
    cosine = np.cos(angle) / np.sqrt(points)
    sine = np.sin(angle) / np.sqrt(points)
    real_row = np.concatenate([cosine, sine], axis=2)
    imag_row = np.concatenate([-sine, cosine], axis=2)
    table = np.stack([real_row, imag_row], axis=2).reshape(per_device, -1, points)
    table = table.astype(np.float32)
    high = table.astype(ml_dtypes.bfloat16)
    low = (table - high.astype(np.float32)).astype(ml_dtypes.bfloat16)
    return np.concatenate([high, high, low], axis=2)


def channelize_kernel(
    frames, spectra, tap_count, group, x_ref, taps_ref, table_ref, out_ref, lined, windowed, turned, packed, sent
):
    step = pl.program_id(0)
    rows = x_ref.shape[0] // group
    per_frame = rows // frames
    segment = spectra // 8
    span = segment * per_frame
    needed = (segment + tap_count - 1) * per_frame
    pitch = lined.shape[0] // group
    half_taps = tap_count // 2
    pairs = segment // 2

    for member in range(group):
        for lane in range(8):
            count = min(-(-needed // 8) * 8, rows - lane * span)
            start = member * rows + lane * span
            values = x_ref[start : start + count, :].astype(jnp.float32)
            lined[pl.ds(member * pitch + lane, count, stride=8), :] = values

    def window(member, part):
        half = part // 2
        columns = slice(half * LANES, (half + 1) * LANES)
        taps = [jnp.broadcast_to(taps_ref[t : t + 1, columns], (8, LANES)) for t in range(tap_count)]
        even, odd = taps[0::2], taps[1::2]
        both = [first + second for first, second in zip(even, odd)]

        def frame(index):
            start = member * pitch + (per_frame * index + part) * 8
            return lined[start : start + 8, :]

        def put(index, values):
            row = member * spectra + index * 8
            windowed[row : row + 8, part * LANES : (part + 1) * LANES] = values

        def feed(totals, factors, values, index, count):
            for tap in range(half_taps):
                target = index - tap
                if 0 <= target < count:
                    term = factors[tap] * values
                    totals[target] = totals[target] + term if target in totals else term

        evens, odds, sums = {}, {}, {}
        late = None
        for index in range(pairs + half_taps):
            early = frame(2 * index)
            feed(evens, even, early, index, pairs + 1)
            if index > 0:
                feed(odds, odd, late, index - 1, pairs)
                feed(sums, both, late + early, index - 1, pairs)
                done = index - half_taps
                if done >= 0:
                    second = odds.pop(done)
                    put(2 * done, evens[done] + second)
                    put(2 * done + 1, sums.pop(done) - (evens[done + 1] + second))
                    evens.pop(done)
            if index < pairs + half_taps - 1:
                late = frame(2 * index + 1)

    contract = (((1,), (1,)), ((), ()))
    parities, outputs, points = table_ref.shape[0], table_ref.shape[1], windowed.shape[1]
    inputs_here = turned.shape[1] // (parities * outputs)
    batch = BATCH
    for first in range(0, group, batch):
        for member in range(first, first + batch):
            for part in range(per_frame):
                window(member, part)
        rows = slice(first * spectra, (first + batch) * spectra)
        near = windowed[rows, : points // 2]
        far = windowed[rows, points // 2 :]
        for parity in range(parities):
            folded = near + far if parity == 0 else near - far
            high = folded.astype(jnp.bfloat16)
            low = (folded - high.astype(jnp.float32)).astype(jnp.bfloat16)
            spectrum = lax.dot_general(
                table_ref[parity],
                jnp.concatenate([high, low, high], axis=1),
                contract,
                preferred_element_type=jnp.float32,
            )
            for member in range(batch):
                start = parity * outputs * inputs_here + step * group + first + member
                for column in range(spectra // LANES):
                    left = member * spectra + column * LANES
                    turned[column, pl.ds(start, outputs, stride=inputs_here), :] = spectrum[
                        :, left : left + LANES
                    ]

    @pl.when(step == pl.num_programs(0) - 1)
    def _():
        chunks = sent.shape[0]
        owners = packed.shape[0] // chunks
        count = outputs * inputs_here // chunks
        copies = []
        for chunk in range(chunks):
            here = slice(chunk * owners, (chunk + 1) * owners)
            for column in range(spectra // LANES):
                columns = slice(column * LANES, (column + 1) * LANES)
                for parity in range(parities):
                    start = (parity * chunks + chunk) * count
                    values = turned[column, start : start + count, :].astype(jnp.bfloat16)
                    packed[here, parity, :, columns] = values.reshape(owners, -1, LANES)
            copies.append(pltpu.make_async_copy(packed.at[here], out_ref.at[here], sent.at[chunk]))
            copies[-1].start()
        for copy in copies:
            copy.wait()


def channelize(samples, filter_taps, owners):
    inputs_here, _, length = samples.shape
    tap_count, points = filter_taps.shape
    frames = length // points
    spectra = frames - tap_count + 1
    halves = points // LANES
    group = 4
    table = fourier_table(points, owners)
    lined = samples.reshape(inputs_here, 2, frames, halves, LANES).transpose(0, 2, 3, 1, 4)
    lined = lined.reshape(-1, LANES)
    rows = lined.shape[0] // inputs_here * group
    shape = (owners, points // owners, 2 * inputs_here, spectra)
    pitch = -(-(spectra // 8 + tap_count - 1) * 2 * halves // 8) * 64
    whole = lambda array: pl.BlockSpec(array.shape, lambda i: (0,) * array.ndim)
    voltage = pl.pallas_call(
        functools.partial(channelize_kernel, frames, spectra, tap_count, group),
        out_shape=jax.ShapeDtypeStruct(shape, jnp.bfloat16),
        grid=(inputs_here // group,),
        in_specs=[
            pl.BlockSpec((rows, LANES), lambda i: (i, 0)),
            whole(filter_taps),
            whole(table),
        ],
        out_specs=pl.BlockSpec(memory_space=pl.ANY),
        scratch_shapes=[
            pltpu.VMEM((group * pitch, LANES), jnp.float32),
            pltpu.VMEM((group * spectra, 2 * points), jnp.float32),
            pltpu.VMEM((spectra // LANES, 2 * points * inputs_here, LANES), jnp.float32),
            pltpu.VMEM(shape, jnp.bfloat16),
            pltpu.SemaphoreType.DMA((4,)),
        ],
        compiler_params=pltpu.CompilerParams(vmem_limit_bytes=60 << 20),
        name="channelize",
    )(lined, filter_taps, jnp.asarray(table))
    return voltage.reshape(owners, points // owners, 2, inputs_here, spectra)


def beam_kernel(scale, volt_ref, weight_ref, out_ref, held, arrived):
    inner, outer, per_device, _, inputs, spectra = volt_ref.shape
    pols, beams = weight_ref.shape[1], weight_ref.shape[-1]
    each = outer // pols
    dishes = each * inner * inputs
    owners, chunk = out_ref.shape[0], out_ref.shape[-1]

    def gathered(channel, pol, part):
        blocks = [
            volt_ref[:, source, channel, part].reshape(inner * inputs, spectra)
            for source in range(pol * each, (pol + 1) * each)
        ]
        return jnp.concatenate(blocks, axis=0).T

    copies = {}
    for channel in range(per_device):
        for pol in range(pols):
            copies[channel, pol] = pltpu.make_async_copy(
                weight_ref.at[channel, pol], held.at[channel, pol], arrived.at[channel, pol]
            )
            copies[channel, pol].start()
    for channel in range(per_device):
        total = None
        for pol in range(pols):
            real = gathered(channel, pol, 0)
            imag = gathered(channel, pol, 1)
            lhs = jnp.concatenate(
                [jnp.concatenate([real, -imag], axis=1), jnp.concatenate([imag, real], axis=1)], axis=0
            )
            copies[channel, pol].wait()
            weights = held[channel, pol].reshape(2 * dishes, beams)
            formed = jnp.dot(lhs, weights, preferred_element_type=jnp.float32)
            power = formed * formed
            power = power[:spectra] + power[spectra:]
            power = power.reshape(spectra // (8 * INTEG), INTEG, 8, beams).sum(axis=1)
            total = power if total is None else total + power
        total = (total.reshape(spectra // INTEG, beams) * jnp.float32(scale)).astype(jnp.bfloat16)
        for owner in range(owners):
            out_ref[owner, channel] = total[:, owner * chunk : (owner + 1) * chunk]


def beam_power(turned, weights, wide_count):
    per_device, spectra = turned.shape[2], turned.shape[5]
    pols, beams = weights.shape[1], weights.shape[4]
    bins = spectra // INTEG
    vmem = pl.BlockSpec(memory_space=pltpu.VMEM)
    return pl.pallas_call(
        functools.partial(beam_kernel, 1.0 / (pols * INTEG)),
        out_shape=jax.ShapeDtypeStruct((wide_count, per_device, bins, beams // wide_count), jnp.bfloat16),
        in_specs=[vmem, pl.BlockSpec(memory_space=pl.ANY)],
        out_specs=vmem,
        scratch_shapes=[
            pltpu.VMEM(weights.shape, weights.dtype),
            pltpu.SemaphoreType.DMA((per_device, pols)),
        ],
        compiler_params=pltpu.CompilerParams(vmem_limit_bytes=50 << 20),
        name="beam_power",
    )(turned, weights)


def band_kernel(odd_ref, row_ref, out_ref):
    bins, width = row_ref.shape
    block = out_ref.shape[0]
    odd = odd_ref[0] > 0
    for channel in range(block // bins):
        rows = slice(channel * bins, (channel + 1) * bins)
        shifted = pltpu.roll(row_ref[...], channel * bins, axis=1)
        low, high = shifted[:, :block], shifted[:, width - block :]
        out_ref[rows, :block] = jnp.where(odd, low, high).astype(jnp.bfloat16)
        out_ref[rows, block : width - block] = shifted[:, block : width - block].astype(jnp.bfloat16)
        out_ref[rows, width - block :] = jnp.where(odd, high, low).astype(jnp.bfloat16)


def banded(smooth_kernel, odd, channels_here, bins):
    extent = smooth_kernel.shape[0]
    half = extent // 2
    stored = np.arange(bins) // 8 + np.arange(bins) % 8 * (bins // 8)
    distance = stored[None, :] - np.arange(bins)[:, None] + half
    selector = (distance[None] == np.arange(extent)[:, None, None]).astype(ml_dtypes.bfloat16)
    row = jnp.einsum(
        "dtu,kd->tku",
        jnp.asarray(selector),
        smooth_kernel.astype(jnp.bfloat16),
        preferred_element_type=jnp.float32,
    ).reshape(bins, extent * bins)
    width = (channels_here + extent - 1) * bins
    row = jnp.pad(row, ((0, 0), (0, width - extent * bins)))
    vmem = pl.BlockSpec(memory_space=pltpu.VMEM)
    return pl.pallas_call(
        band_kernel,
        out_shape=jax.ShapeDtypeStruct((channels_here * bins, width), jnp.bfloat16),
        in_specs=[pl.BlockSpec(memory_space=pltpu.SMEM), vmem],
        out_specs=vmem,
        compiler_params=pltpu.CompilerParams(vmem_limit_bytes=16 << 20),
        name="band",
    )(odd.astype(jnp.int32).reshape(1), row)


def filtered(refs, matrix):
    centered = []
    for ref in refs:
        channels, bins, beams = ref.shape
        values = ref[...].astype(jnp.float32)
        values = values - jnp.mean(values, axis=1, keepdims=True)
        centered.append(values.astype(jnp.bfloat16).reshape(channels * bins, beams))
    stacked = jnp.concatenate(centered, axis=0)
    return jnp.dot(matrix, stacked, preferred_element_type=jnp.float32)


def near_kernel(pair_ref, mid_ref, matrix_ref, out_ref):
    width = out_ref.shape[0]
    out_ref[...] = filtered((pair_ref, mid_ref), matrix_ref[:, : 2 * width])


def far_kernel(other_ref, part_ref, matrix_ref, out_ref):
    width = part_ref.shape[0]
    result = part_ref[...] + filtered((other_ref,), matrix_ref[:, 2 * width :])
    out_ref[...] = result.reshape(out_ref.shape)


def smooth(pair, mid, other, matrix):
    channels, bins, beams = mid.shape
    vmem = pl.BlockSpec(memory_space=pltpu.VMEM)
    near = pl.pallas_call(
        near_kernel,
        out_shape=jax.ShapeDtypeStruct((channels * bins, beams), jnp.float32),
        in_specs=[vmem] * 3,
        out_specs=vmem,
        compiler_params=pltpu.CompilerParams(vmem_limit_bytes=16 << 20),
        name="smooth_near",
    )(pair, mid, matrix)
    return pl.pallas_call(
        far_kernel,
        out_shape=jax.ShapeDtypeStruct(mid.shape, jnp.float32),
        in_specs=[vmem] * 3,
        out_specs=vmem,
        compiler_params=pltpu.CompilerParams(vmem_limit_bytes=16 << 20),
        name="smooth_far",
    )(other, near, matrix)


def body(samples, filter_taps, beam_weights, smooth_kernel):
    wide_count = lax.axis_size("wide")
    narrow_count = lax.axis_size("narrow")
    voltage = channelize(samples, filter_taps, wide_count * narrow_count)
    voltage, smooth_kernel = lax.optimization_barrier((voltage, smooth_kernel))
    turned = lax.all_to_all(voltage, ("narrow", "wide"), split_axis=0, concat_axis=0, tiled=True)
    turned = turned.reshape(narrow_count, wide_count, *turned.shape[1:])
    per_device, spectra = turned.shape[2], turned.shape[5]
    odd = lax.axis_index("narrow") % 2
    matrix = banded(smooth_kernel, odd, per_device * wide_count, spectra // INTEG)
    turned, matrix = lax.optimization_barrier((turned, matrix))
    intensity = beam_power(turned, beam_weights, wide_count)
    bins, beams = intensity.shape[2], intensity.shape[3]
    by_beam = lax.all_to_all(intensity, "wide", split_axis=0, concat_axis=0, tiled=True)
    by_beam = by_beam.reshape(-1, bins, beams)
    pairs = [(i, i ^ 1) for i in range(narrow_count)]
    others = [(i, i - 1 + i % 2 * 2) for i in range(1, narrow_count - 1)]
    other = lax.ppermute(by_beam, "narrow", others)
    pair = lax.ppermute(by_beam, "narrow", pairs)
    return smooth(pair, by_beam, other, matrix)


def solution(mesh):
    placed = (
        P(("wide", "narrow"), None, None),
        P(),
        P(("narrow", "wide"), None, None, None, None),
        P(),
    )
    return jax.shard_map(
        body, mesh=mesh, in_specs=placed, out_specs=P("narrow", None, "wide"), check_vma=False
    )
```

```python
import functools

import jax
import jax.numpy as jnp
import ml_dtypes
import numpy as np
from jax import lax
from jax.experimental import pallas as pl
from jax.experimental.pallas import tpu as pltpu
from jax.sharding import PartitionSpec as P

INTEG = 8
HALF = 16
LANES = 128
BATCH = 2


def fourier_table(points, owners):
    per_device = points // owners
    first = np.arange(owners) * per_device
    channel = first[None, :] + np.arange(per_device)[:, None]
    angle = (channel[:, :, None] * np.arange(points // 2) % points) * (2.0 * np.pi / points)
    cosine = np.cos(angle) / np.sqrt(points)
    sine = np.sin(angle) / np.sqrt(points)
    real_row = np.concatenate([cosine, sine], axis=2)
    imag_row = np.concatenate([-sine, cosine], axis=2)
    table = np.stack([real_row, imag_row], axis=2).reshape(per_device, -1, points)
    table = table.astype(np.float32)
    high = table.astype(ml_dtypes.bfloat16)
    low = (table - high.astype(np.float32)).astype(ml_dtypes.bfloat16)
    return np.concatenate([high, high, low], axis=2)


def channelize_kernel(
    frames, spectra, tap_count, group, x_ref, taps_ref, table_ref, out_ref, lined, windowed, turned, packed, sent
):
    step = pl.program_id(0)
    rows = x_ref.shape[0] // group
    per_frame = rows // frames
    segment = spectra // 8
    span = segment * per_frame
    needed = (segment + tap_count - 1) * per_frame
    pitch = lined.shape[0] // group
    half_taps = tap_count // 2
    pairs = segment // 2

    for member in range(group):
        for lane in range(8):
            count = min(-(-needed // 8) * 8, rows - lane * span)
            start = member * rows + lane * span
            values = x_ref[start : start + count, :].astype(jnp.float32)
            lined[pl.ds(member * pitch + lane, count, stride=8), :] = values

    def window(member, part):
        half = part // 2
        columns = slice(half * LANES, (half + 1) * LANES)
        taps = [jnp.broadcast_to(taps_ref[t : t + 1, columns], (8, LANES)) for t in range(tap_count)]
        even, odd = taps[0::2], taps[1::2]
        both = [first + second for first, second in zip(even, odd)]

        def frame(index):
            start = member * pitch + (per_frame * index + part) * 8
            return lined[start : start + 8, :]

        def put(index, values):
            row = member * spectra + index * 8
            windowed[row : row + 8, part * LANES : (part + 1) * LANES] = values

        def feed(totals, factors, values, index, count):
            for tap in range(half_taps):
                target = index - tap
                if 0 <= target < count:
                    term = factors[tap] * values
                    totals[target] = totals[target] + term if target in totals else term

        evens, odds, sums = {}, {}, {}
        late = None
        for index in range(pairs + half_taps):
            early = frame(2 * index)
            feed(evens, even, early, index, pairs + 1)
            if index > 0:
                feed(odds, odd, late, index - 1, pairs)
                feed(sums, both, late + early, index - 1, pairs)
                done = index - half_taps
                if done >= 0:
                    second = odds.pop(done)
                    put(2 * done, evens[done] + second)
                    put(2 * done + 1, sums.pop(done) - (evens[done + 1] + second))
                    evens.pop(done)
            if index < pairs + half_taps - 1:
                late = frame(2 * index + 1)

    contract = (((1,), (1,)), ((), ()))
    parities, outputs, points = table_ref.shape[0], table_ref.shape[1], windowed.shape[1]
    inputs_here = turned.shape[1] // (parities * outputs)
    batch = BATCH
    for first in range(0, group, batch):
        for member in range(first, first + batch):
            for part in range(per_frame):
                window(member, part)
        rows = slice(first * spectra, (first + batch) * spectra)
        near = windowed[rows, : points // 2]
        far = windowed[rows, points // 2 :]
        for parity in range(parities):
            folded = near + far if parity == 0 else near - far
            high = folded.astype(jnp.bfloat16)
            low = (folded - high.astype(jnp.float32)).astype(jnp.bfloat16)
            spectrum = lax.dot_general(
                table_ref[parity],
                jnp.concatenate([high, low, high], axis=1),
                contract,
                preferred_element_type=jnp.float32,
            )
            for member in range(batch):
                start = parity * outputs * inputs_here + step * group + first + member
                for column in range(spectra // LANES):
                    left = member * spectra + column * LANES
                    turned[column, pl.ds(start, outputs, stride=inputs_here), :] = spectrum[
                        :, left : left + LANES
                    ]

    @pl.when(step == pl.num_programs(0) - 1)
    def _():
        chunks = sent.shape[0]
        owners = packed.shape[0] // chunks
        count = outputs * inputs_here // chunks
        copies = []
        for chunk in range(chunks):
            here = slice(chunk * owners, (chunk + 1) * owners)
            for column in range(spectra // LANES):
                columns = slice(column * LANES, (column + 1) * LANES)
                for parity in range(parities):
                    start = (parity * chunks + chunk) * count
                    values = turned[column, start : start + count, :].astype(jnp.bfloat16)
                    packed[here, parity, :, columns] = values.reshape(owners, -1, LANES)
            copies.append(pltpu.make_async_copy(packed.at[here], out_ref.at[here], sent.at[chunk]))
            copies[-1].start()
        for copy in copies:
            copy.wait()


def channelize(samples, filter_taps, owners):
    inputs_here, _, length = samples.shape
    tap_count, points = filter_taps.shape
    frames = length // points
    spectra = frames - tap_count + 1
    halves = points // LANES
    group = 4
    table = fourier_table(points, owners)
    lined = samples.reshape(inputs_here, 2, frames, halves, LANES).transpose(0, 2, 3, 1, 4)
    lined = lined.reshape(-1, LANES)
    rows = lined.shape[0] // inputs_here * group
    shape = (owners, points // owners, 2 * inputs_here, spectra)
    pitch = -(-(spectra // 8 + tap_count - 1) * 2 * halves // 8) * 64
    whole = lambda array: pl.BlockSpec(array.shape, lambda i: (0,) * array.ndim)
    voltage = pl.pallas_call(
        functools.partial(channelize_kernel, frames, spectra, tap_count, group),
        out_shape=jax.ShapeDtypeStruct(shape, jnp.bfloat16),
        grid=(inputs_here // group,),
        in_specs=[
            pl.BlockSpec((rows, LANES), lambda i: (i, 0)),
            whole(filter_taps),
            whole(table),
        ],
        out_specs=pl.BlockSpec(memory_space=pl.ANY),
        scratch_shapes=[
            pltpu.VMEM((group * pitch, LANES), jnp.float32),
            pltpu.VMEM((group * spectra, 2 * points), jnp.float32),
            pltpu.VMEM((spectra // LANES, 2 * points * inputs_here, LANES), jnp.float32),
            pltpu.VMEM(shape, jnp.bfloat16),
            pltpu.SemaphoreType.DMA((4,)),
        ],
        compiler_params=pltpu.CompilerParams(vmem_limit_bytes=60 << 20),
        name="channelize",
    )(lined, filter_taps, jnp.asarray(table))
    return voltage.reshape(owners, points // owners, 2, inputs_here, spectra)


def beam_kernel(scale, volt_ref, weight_ref, out_ref, held, arrived):
    inner, outer, per_device, _, inputs, spectra = volt_ref.shape
    pols, beams = weight_ref.shape[1], weight_ref.shape[-1]
    each = outer // pols
    dishes = each * inner * inputs
    owners, chunk = out_ref.shape[0], out_ref.shape[-1]

    def gathered(channel, pol, part):
        blocks = [
            volt_ref[:, source, channel, part].reshape(inner * inputs, spectra)
            for source in range(pol * each, (pol + 1) * each)
        ]
        return jnp.concatenate(blocks, axis=0).T

    copies = {}
    for channel in range(per_device):
        for pol in range(pols):
            copies[channel, pol] = pltpu.make_async_copy(
                weight_ref.at[channel, pol], held.at[channel, pol], arrived.at[channel, pol]
            )
            copies[channel, pol].start()
    for channel in range(per_device):
        total = None
        for pol in range(pols):
            real = gathered(channel, pol, 0)
            imag = gathered(channel, pol, 1)
            lhs = jnp.concatenate(
                [jnp.concatenate([real, -imag], axis=1), jnp.concatenate([imag, real], axis=1)], axis=0
            )
            copies[channel, pol].wait()
            weights = held[channel, pol].reshape(2 * dishes, beams)
            formed = jnp.dot(lhs, weights, preferred_element_type=jnp.float32)
            power = formed * formed
            power = power[:spectra] + power[spectra:]
            power = power.reshape(spectra // (8 * INTEG), INTEG, 8, beams).sum(axis=1)
            total = power if total is None else total + power
        total = (total.reshape(spectra // INTEG, beams) * jnp.float32(scale)).astype(jnp.bfloat16)
        for owner in range(owners):
            values = total[:, owner * chunk : (owner + 1) * chunk]
            out_ref[owner, 0, channel] = values
            out_ref[owner ^ 1, 1, channel] = values


def beam_power(turned, weights, wide_count):
    per_device, spectra = turned.shape[2], turned.shape[5]
    pols, beams = weights.shape[1], weights.shape[4]
    bins = spectra // INTEG
    vmem = pl.BlockSpec(memory_space=pltpu.VMEM)
    return pl.pallas_call(
        functools.partial(beam_kernel, 1.0 / (pols * INTEG)),
        out_shape=jax.ShapeDtypeStruct((wide_count, 2, per_device, bins, beams // wide_count), jnp.bfloat16),
        in_specs=[vmem, pl.BlockSpec(memory_space=pl.ANY)],
        out_specs=vmem,
        scratch_shapes=[
            pltpu.VMEM(weights.shape, weights.dtype),
            pltpu.SemaphoreType.DMA((per_device, pols)),
        ],
        compiler_params=pltpu.CompilerParams(vmem_limit_bytes=50 << 20),
        name="beam_power",
    )(turned, weights)


def band_kernel(odd_ref, row_ref, out_ref):
    bins, width = row_ref.shape
    block = out_ref.shape[0]
    odd = odd_ref[0] > 0
    for channel in range(block // bins):
        rows = slice(channel * bins, (channel + 1) * bins)
        shifted = pltpu.roll(row_ref[...], channel * bins, axis=1)
        low, high = shifted[:, :block], shifted[:, width - block :]
        out_ref[rows, :block] = jnp.where(odd, low, high).astype(jnp.bfloat16)
        out_ref[rows, block : width - block] = shifted[:, block : width - block].astype(jnp.bfloat16)
        out_ref[rows, width - block :] = jnp.where(odd, high, low).astype(jnp.bfloat16)


def banded(smooth_kernel, odd, channels_here, bins):
    extent = smooth_kernel.shape[0]
    half = extent // 2
    stored = np.arange(bins) // 8 + np.arange(bins) % 8 * (bins // 8)
    distance = stored[None, :] - np.arange(bins)[:, None] + half
    selector = (distance[None] == np.arange(extent)[:, None, None]).astype(ml_dtypes.bfloat16)
    row = jnp.einsum(
        "dtu,kd->tku",
        jnp.asarray(selector),
        smooth_kernel.astype(jnp.bfloat16),
        preferred_element_type=jnp.float32,
    ).reshape(bins, extent * bins)
    width = (channels_here + extent - 1) * bins
    row = jnp.pad(row, ((0, 0), (0, width - extent * bins)))
    vmem = pl.BlockSpec(memory_space=pltpu.VMEM)
    return pl.pallas_call(
        band_kernel,
        out_shape=jax.ShapeDtypeStruct((channels_here * bins, width), jnp.bfloat16),
        in_specs=[pl.BlockSpec(memory_space=pltpu.SMEM), vmem],
        out_specs=vmem,
        compiler_params=pltpu.CompilerParams(vmem_limit_bytes=16 << 20),
        name="band",
    )(odd.astype(jnp.int32).reshape(1), row)


def filtered(refs, matrix):
    centered = []
    for ref in refs:
        channels, bins, beams = ref.shape
        values = ref[...].astype(jnp.float32)
        values = values - jnp.mean(values, axis=1, keepdims=True)
        centered.append(values.astype(jnp.bfloat16).reshape(channels * bins, beams))
    stacked = jnp.concatenate(centered, axis=0)
    return jnp.dot(matrix, stacked, preferred_element_type=jnp.float32)


def near_kernel(pair_ref, mid_ref, matrix_ref, out_ref):
    width = out_ref.shape[0]
    out_ref[...] = filtered((pair_ref, mid_ref), matrix_ref[:, : 2 * width])


def far_kernel(other_ref, part_ref, matrix_ref, out_ref):
    width = part_ref.shape[0]
    result = part_ref[...] + filtered((other_ref,), matrix_ref[:, 2 * width :])
    out_ref[...] = result.reshape(out_ref.shape)


def smooth(pair, mid, other, matrix):
    channels, bins, beams = mid.shape
    vmem = pl.BlockSpec(memory_space=pltpu.VMEM)
    near = pl.pallas_call(
        near_kernel,
        out_shape=jax.ShapeDtypeStruct((channels * bins, beams), jnp.float32),
        in_specs=[vmem] * 3,
        out_specs=vmem,
        compiler_params=pltpu.CompilerParams(vmem_limit_bytes=16 << 20),
        name="smooth_near",
    )(pair, mid, matrix)
    return pl.pallas_call(
        far_kernel,
        out_shape=jax.ShapeDtypeStruct(mid.shape, jnp.float32),
        in_specs=[vmem] * 3,
        out_specs=vmem,
        compiler_params=pltpu.CompilerParams(vmem_limit_bytes=16 << 20),
        name="smooth_far",
    )(other, near, matrix)


def body(samples, filter_taps, beam_weights, smooth_kernel):
    wide_count = lax.axis_size("wide")
    narrow_count = lax.axis_size("narrow")
    voltage = channelize(samples, filter_taps, wide_count * narrow_count)
    voltage, smooth_kernel = lax.optimization_barrier((voltage, smooth_kernel))
    turned = lax.all_to_all(voltage, ("narrow", "wide"), split_axis=0, concat_axis=0, tiled=True)
    turned = turned.reshape(narrow_count, wide_count, *turned.shape[1:])
    per_device, spectra = turned.shape[2], turned.shape[5]
    odd = lax.axis_index("narrow") % 2
    matrix = banded(smooth_kernel, odd, per_device * wide_count, spectra // INTEG)
    turned, matrix = lax.optimization_barrier((turned, matrix))
    intensity = beam_power(turned, beam_weights, wide_count)
    bins, beams = intensity.shape[3], intensity.shape[4]
    by_beam = lax.all_to_all(intensity, "wide", split_axis=0, concat_axis=0, tiled=True)
    own = by_beam[:, 0].reshape(-1, bins, beams)
    lent = by_beam[:, 1].reshape(-1, bins, beams)
    pairs = [(i, i ^ 1) for i in range(narrow_count)]
    others = [
        (w * narrow_count + i, (w ^ 1) * narrow_count + i - 1 + i % 2 * 2)
        for i in range(1, narrow_count - 1)
        for w in range(wide_count)
    ]
    other = lax.ppermute(lent, ("wide", "narrow"), others)
    pair = lax.ppermute(own, "narrow", pairs)
    return smooth(pair, own, other, matrix)


def solution(mesh):
    placed = (
        P(("wide", "narrow"), None, None),
        P(),
        P(("narrow", "wide"), None, None, None, None),
        P(),
    )
    return jax.shard_map(
        body, mesh=mesh, in_specs=placed, out_specs=P("narrow", None, "wide"), check_vma=False
    )
```

```python
import functools

import jax
import jax.numpy as jnp
import ml_dtypes
import numpy as np
from jax import lax
from jax.experimental import pallas as pl
from jax.experimental.pallas import tpu as pltpu
from jax.sharding import PartitionSpec as P

INTEG = 8
HALF = 16
LANES = 128
BATCH = 2


def fourier_table(points, owners):
    per_device = points // owners
    first = np.arange(owners) * per_device
    channel = first[None, :] + np.arange(per_device)[:, None]
    angle = (channel[:, :, None] * np.arange(points // 2) % points) * (2.0 * np.pi / points)
    cosine = np.cos(angle) / np.sqrt(points)
    sine = np.sin(angle) / np.sqrt(points)
    real_row = np.concatenate([cosine, sine], axis=2)
    imag_row = np.concatenate([-sine, cosine], axis=2)
    table = np.stack([real_row, imag_row], axis=2).reshape(per_device, -1, points)
    table = table.astype(np.float32)
    high = table.astype(ml_dtypes.bfloat16)
    low = (table - high.astype(np.float32)).astype(ml_dtypes.bfloat16)
    return np.concatenate([high, high, low], axis=2)


def channelize_kernel(
    frames, spectra, tap_count, group, x_ref, taps_ref, table_ref, out_ref, lined, windowed, turned, packed, sent
):
    step = pl.program_id(0)
    rows = x_ref.shape[0] // group
    per_frame = rows // frames
    segment = spectra // 8
    span = segment * per_frame
    needed = (segment + tap_count - 1) * per_frame
    pitch = lined.shape[0] // group
    half_taps = tap_count // 2
    pairs = segment // 2

    for member in range(group):
        for lane in range(8):
            count = min(-(-needed // 8) * 8, rows - lane * span)
            start = member * rows + lane * span
            values = x_ref[start : start + count, :].astype(jnp.float32)
            lined[pl.ds(member * pitch + lane, count, stride=8), :] = values

    def window(member, part):
        half = part // 2
        columns = slice(half * LANES, (half + 1) * LANES)
        taps = [jnp.broadcast_to(taps_ref[t : t + 1, columns], (8, LANES)) for t in range(tap_count)]
        even, odd = taps[0::2], taps[1::2]
        both = [first + second for first, second in zip(even, odd)]

        def frame(index):
            start = member * pitch + (per_frame * index + part) * 8
            return lined[start : start + 8, :]

        def put(index, values):
            row = member * spectra + index * 8
            windowed[row : row + 8, part * LANES : (part + 1) * LANES] = values

        def feed(totals, factors, values, index, count):
            for tap in range(half_taps):
                target = index - tap
                if 0 <= target < count:
                    term = factors[tap] * values
                    totals[target] = totals[target] + term if target in totals else term

        evens, odds, sums = {}, {}, {}
        late = None
        for index in range(pairs + half_taps):
            early = frame(2 * index)
            feed(evens, even, early, index, pairs + 1)
            if index > 0:
                feed(odds, odd, late, index - 1, pairs)
                feed(sums, both, late + early, index - 1, pairs)
                done = index - half_taps
                if done >= 0:
                    second = odds.pop(done)
                    put(2 * done, evens[done] + second)
                    put(2 * done + 1, sums.pop(done) - (evens[done + 1] + second))
                    evens.pop(done)
            if index < pairs + half_taps - 1:
                late = frame(2 * index + 1)

    contract = (((1,), (1,)), ((), ()))
    parities, outputs, points = table_ref.shape[0], table_ref.shape[1], windowed.shape[1]
    inputs_here = turned.shape[1] // (parities * outputs)
    batch = BATCH
    for first in range(0, group, batch):
        for member in range(first, first + batch):
            for part in range(per_frame):
                window(member, part)
        rows = slice(first * spectra, (first + batch) * spectra)
        near = windowed[rows, : points // 2]
        far = windowed[rows, points // 2 :]
        for parity in range(parities):
            folded = near + far if parity == 0 else near - far
            high = folded.astype(jnp.bfloat16)
            low = (folded - high.astype(jnp.float32)).astype(jnp.bfloat16)
            spectrum = lax.dot_general(
                table_ref[parity],
                jnp.concatenate([high, low, high], axis=1),
                contract,
                preferred_element_type=jnp.float32,
            )
            for member in range(batch):
                start = parity * outputs * inputs_here + step * group + first + member
                for column in range(spectra // LANES):
                    left = member * spectra + column * LANES
                    turned[column, pl.ds(start, outputs, stride=inputs_here), :] = spectrum[
                        :, left : left + LANES
                    ]

    @pl.when(step == pl.num_programs(0) - 1)
    def _():
        chunks = sent.shape[0]
        owners = packed.shape[0] // chunks
        count = outputs * inputs_here // chunks
        copies = []
        for chunk in range(chunks):
            here = slice(chunk * owners, (chunk + 1) * owners)
            for column in range(spectra // LANES):
                columns = slice(column * LANES, (column + 1) * LANES)
                for parity in range(parities):
                    start = (parity * chunks + chunk) * count
                    values = turned[column, start : start + count, :].astype(jnp.bfloat16)
                    packed[here, parity, :, columns] = values.reshape(owners, -1, LANES)
            copies.append(pltpu.make_async_copy(packed.at[here], out_ref.at[here], sent.at[chunk]))
            copies[-1].start()
        for copy in copies:
            copy.wait()


def channelize(samples, filter_taps, owners):
    inputs_here, _, length = samples.shape
    tap_count, points = filter_taps.shape
    frames = length // points
    spectra = frames - tap_count + 1
    halves = points // LANES
    group = 4
    table = fourier_table(points, owners)
    lined = samples.reshape(inputs_here, 2, frames, halves, LANES).transpose(0, 2, 3, 1, 4)
    lined = lined.reshape(-1, LANES)
    rows = lined.shape[0] // inputs_here * group
    shape = (owners, points // owners, 2 * inputs_here, spectra)
    pitch = -(-(spectra // 8 + tap_count - 1) * 2 * halves // 8) * 64
    whole = lambda array: pl.BlockSpec(array.shape, lambda i: (0,) * array.ndim)
    voltage = pl.pallas_call(
        functools.partial(channelize_kernel, frames, spectra, tap_count, group),
        out_shape=jax.ShapeDtypeStruct(shape, jnp.bfloat16),
        grid=(inputs_here // group,),
        in_specs=[
            pl.BlockSpec((rows, LANES), lambda i: (i, 0)),
            whole(filter_taps),
            whole(table),
        ],
        out_specs=pl.BlockSpec(memory_space=pl.ANY),
        scratch_shapes=[
            pltpu.VMEM((group * pitch, LANES), jnp.float32),
            pltpu.VMEM((group * spectra, 2 * points), jnp.float32),
            pltpu.VMEM((spectra // LANES, 2 * points * inputs_here, LANES), jnp.float32),
            pltpu.VMEM(shape, jnp.bfloat16),
            pltpu.SemaphoreType.DMA((4,)),
        ],
        compiler_params=pltpu.CompilerParams(vmem_limit_bytes=60 << 20),
        name="channelize",
    )(lined, filter_taps, jnp.asarray(table))
    return voltage.reshape(owners, points // owners, 2, inputs_here, spectra)


def beam_kernel(scale, volt_ref, weight_ref, out_ref, held, arrived):
    inner, outer, per_device, _, inputs, spectra = volt_ref.shape
    pols, beams = weight_ref.shape[1], weight_ref.shape[-1]
    each = outer // pols
    dishes = each * inner * inputs
    owners, chunk = out_ref.shape[0], out_ref.shape[-1]

    def gathered(channel, pol, part):
        blocks = [
            volt_ref[:, source, channel, part].reshape(inner * inputs, spectra)
            for source in range(pol * each, (pol + 1) * each)
        ]
        return jnp.concatenate(blocks, axis=0).T

    copies = {}
    for channel in range(per_device):
        for pol in range(pols):
            copies[channel, pol] = pltpu.make_async_copy(
                weight_ref.at[channel, pol], held.at[channel, pol], arrived.at[channel, pol]
            )
            copies[channel, pol].start()
    for channel in range(per_device):
        total = None
        for pol in range(pols):
            real = gathered(channel, pol, 0)
            imag = gathered(channel, pol, 1)
            lhs = jnp.concatenate(
                [jnp.concatenate([real, -imag], axis=1), jnp.concatenate([imag, real], axis=1)], axis=0
            )
            copies[channel, pol].wait()
            weights = held[channel, pol].reshape(2 * dishes, beams)
            formed = jnp.dot(lhs, weights, preferred_element_type=jnp.float32)
            power = formed * formed
            power = power[:spectra] + power[spectra:]
            power = power.reshape(spectra // (8 * INTEG), INTEG, 8, beams).sum(axis=1)
            total = power if total is None else total + power
        total = (total.reshape(spectra // INTEG, beams) * jnp.float32(scale)).astype(jnp.bfloat16)
        for owner in range(owners):
            out_ref[owner, channel] = total[:, owner * chunk : (owner + 1) * chunk]


def beam_power(turned, weights, wide_count):
    per_device, spectra = turned.shape[2], turned.shape[5]
    pols, beams = weights.shape[1], weights.shape[4]
    bins = spectra // INTEG
    vmem = pl.BlockSpec(memory_space=pltpu.VMEM)
    return pl.pallas_call(
        functools.partial(beam_kernel, 1.0 / (pols * INTEG)),
        out_shape=jax.ShapeDtypeStruct((wide_count, per_device, bins, beams // wide_count), jnp.bfloat16),
        in_specs=[vmem, pl.BlockSpec(memory_space=pl.ANY)],
        out_specs=vmem,
        scratch_shapes=[
            pltpu.VMEM(weights.shape, weights.dtype),
            pltpu.SemaphoreType.DMA((per_device, pols)),
        ],
        compiler_params=pltpu.CompilerParams(vmem_limit_bytes=50 << 20),
        name="beam_power",
    )(turned, weights)


def band_kernel(odd_ref, row_ref, out_ref):
    bins, width = row_ref.shape
    block = out_ref.shape[0]
    odd = odd_ref[0] > 0
    for channel in range(block // bins):
        rows = slice(channel * bins, (channel + 1) * bins)
        shifted = pltpu.roll(row_ref[...], channel * bins, axis=1)
        low, high = shifted[:, :block], shifted[:, width - block :]
        out_ref[rows, :block] = shifted[:, block : width - block].astype(jnp.bfloat16)
        out_ref[rows, block : width - block] = jnp.where(odd, low, high).astype(jnp.bfloat16)
        out_ref[rows, width - block :] = jnp.where(odd, high, low).astype(jnp.bfloat16)


def banded(smooth_kernel, odd, channels_here, bins):
    extent = smooth_kernel.shape[0]
    half = extent // 2
    stored = np.arange(bins) // 8 + np.arange(bins) % 8 * (bins // 8)
    distance = stored[None, :] - np.arange(bins)[:, None] + half
    selector = (distance[None] == np.arange(extent)[:, None, None]).astype(ml_dtypes.bfloat16)
    row = jnp.einsum(
        "dtu,kd->tku",
        jnp.asarray(selector),
        smooth_kernel.astype(jnp.bfloat16),
        preferred_element_type=jnp.float32,
    ).reshape(bins, extent * bins)
    width = (channels_here + extent - 1) * bins
    row = jnp.pad(row, ((0, 0), (0, width - extent * bins)))
    vmem = pl.BlockSpec(memory_space=pltpu.VMEM)
    return pl.pallas_call(
        band_kernel,
        out_shape=jax.ShapeDtypeStruct((channels_here * bins, width), jnp.bfloat16),
        in_specs=[pl.BlockSpec(memory_space=pltpu.SMEM), vmem],
        out_specs=vmem,
        compiler_params=pltpu.CompilerParams(vmem_limit_bytes=16 << 20),
        name="band",
    )(odd.astype(jnp.int32).reshape(1), row)


def filtered(refs, matrix):
    centered = []
    for ref in refs:
        channels, bins, beams = ref.shape
        values = ref[...].astype(jnp.float32)
        values = values - jnp.mean(values, axis=1, keepdims=True)
        centered.append(values.astype(jnp.bfloat16).reshape(channels * bins, beams))
    stacked = jnp.concatenate(centered, axis=0)
    return jnp.dot(matrix, stacked, preferred_element_type=jnp.float32)


def near_kernel(mid_ref, matrix_ref, out_ref):
    width = out_ref.shape[0]
    out_ref[...] = filtered((mid_ref,), matrix_ref[:, :width])


def far_kernel(other_ref, pair_ref, part_ref, matrix_ref, out_ref):
    width = part_ref.shape[0]
    result = part_ref[...] + filtered((pair_ref, other_ref), matrix_ref[:, width:])
    out_ref[...] = result.reshape(out_ref.shape)


def smooth(pair, mid, other, matrix):
    channels, bins, beams = mid.shape
    vmem = pl.BlockSpec(memory_space=pltpu.VMEM)
    near = pl.pallas_call(
        near_kernel,
        out_shape=jax.ShapeDtypeStruct((channels * bins, beams), jnp.float32),
        in_specs=[vmem] * 2,
        out_specs=vmem,
        compiler_params=pltpu.CompilerParams(vmem_limit_bytes=16 << 20),
        name="smooth_near",
    )(mid, matrix)
    return pl.pallas_call(
        far_kernel,
        out_shape=jax.ShapeDtypeStruct(mid.shape, jnp.float32),
        in_specs=[vmem] * 4,
        out_specs=vmem,
        compiler_params=pltpu.CompilerParams(vmem_limit_bytes=16 << 20),
        name="smooth_far",
    )(other, pair, near, matrix)


def body(samples, filter_taps, beam_weights, smooth_kernel):
    wide_count = lax.axis_size("wide")
    narrow_count = lax.axis_size("narrow")
    voltage = channelize(samples, filter_taps, wide_count * narrow_count)
    turned = lax.all_to_all(voltage, ("narrow", "wide"), split_axis=0, concat_axis=0, tiled=True)
    turned = turned.reshape(narrow_count, wide_count, *turned.shape[1:])
    per_device, spectra = turned.shape[2], turned.shape[5]
    intensity = beam_power(turned, beam_weights, wide_count)
    intensity, smooth_kernel = lax.optimization_barrier((intensity, smooth_kernel))
    odd = lax.axis_index("narrow") % 2
    matrix = banded(smooth_kernel, odd, per_device * wide_count, spectra // INTEG)
    bins, beams = intensity.shape[2], intensity.shape[3]
    by_beam = lax.all_to_all(intensity, "wide", split_axis=0, concat_axis=0, tiled=True)
    by_beam = by_beam.reshape(-1, bins, beams)
    pairs = [(i, i ^ 1) for i in range(narrow_count)]
    others = [(i, i - 1 + i % 2 * 2) for i in range(1, narrow_count - 1)]
    other = lax.ppermute(by_beam, "narrow", others)
    pair = lax.ppermute(by_beam, "narrow", pairs)
    return smooth(pair, by_beam, other, matrix)


def solution(mesh):
    placed = (
        P(("wide", "narrow"), None, None),
        P(),
        P(("narrow", "wide"), None, None, None, None),
        P(),
    )
    return jax.shard_map(
        body, mesh=mesh, in_specs=placed, out_specs=P("narrow", None, "wide"), check_vma=False
    )
```

```python
import functools

import jax
import jax.numpy as jnp
import ml_dtypes
import numpy as np
from jax import lax
from jax.experimental import pallas as pl
from jax.experimental.pallas import tpu as pltpu
from jax.sharding import PartitionSpec as P

INTEG = 8
HALF = 16
LANES = 128
BATCH = 2
HOIST = 4
WAITS = ((0,), (1, 2, 3))
SHORTEST = 4
PASSES = 3


def fourier_table(points, owners):
    per_device = points // owners
    first = np.arange(owners) * per_device
    channel = first[None, :] + np.arange(per_device)[:, None]
    angle = (channel[:, :, None] * np.arange(points // 2) % points) * (2.0 * np.pi / points)
    cosine = np.cos(angle) / np.sqrt(points)
    sine = np.sin(angle) / np.sqrt(points)
    real_row = np.concatenate([cosine, sine], axis=2)
    imag_row = np.concatenate([-sine, cosine], axis=2)
    table = np.stack([real_row, imag_row], axis=2).reshape(per_device, -1, points)
    table = table.astype(np.float32)
    high = table.astype(ml_dtypes.bfloat16)
    low = (table - high.astype(np.float32)).astype(ml_dtypes.bfloat16)
    return np.concatenate([high, high, low][:PASSES], axis=2)


def fast_filter(taps, value):
    if len(taps) <= SHORTEST:

        def direct(index):
            total = taps[0] * value(index)
            for tap in range(1, len(taps)):
                total = total + taps[tap] * value(index + tap)
            return total

        return direct
    even, odd = taps[0::2], taps[1::2]
    both = [first + second for first, second in zip(even, odd)]
    early = functools.cache(fast_filter(even, lambda index: value(2 * index)))
    late = functools.cache(fast_filter(odd, lambda index: value(2 * index + 1)))
    added = functools.cache(lambda index: value(2 * index + 1) + value(2 * index + 2))
    mixed = functools.cache(fast_filter(both, added))

    def folded(index):
        half = index // 2
        if index % 2 == 0:
            return early(half) + late(half)
        return mixed(half) - (early(half + 1) + late(half))

    return folded


def channelize_kernel(
    frames, spectra, tap_count, group, x_ref, taps_ref, table_ref, out_ref, lined, windowed, turned, packed, sent
):
    step = pl.program_id(0)
    rows = x_ref.shape[0] // group
    per_frame = rows // frames
    segment = spectra // 8
    span = segment * per_frame
    needed = (segment + tap_count - 1) * per_frame
    pitch = lined.shape[0] // group

    for member in range(group):
        for lane in range(8):
            count = min(-(-needed // 8) * 8, rows - lane * span)
            start = member * rows + lane * span
            values = x_ref[start : start + count, :].astype(jnp.float32)
            lined[pl.ds(member * pitch + lane, count, stride=8), :] = values

    def window(member, part):
        half = part // 2
        columns = slice(half * LANES, (half + 1) * LANES)
        taps = [jnp.broadcast_to(taps_ref[t : t + 1, columns], (8, LANES)) for t in range(tap_count)]

        def frame(index):
            start = member * pitch + (per_frame * index + part) * 8
            return lined[start : start + 8, :]

        filtered = fast_filter(taps, frame)
        for index in range(segment):
            row = member * spectra + index * 8
            windowed[row : row + 8, part * LANES : (part + 1) * LANES] = filtered(index)

    contract = (((1,), (1,)), ((), ()))
    parities, outputs, points = table_ref.shape[0], table_ref.shape[1], windowed.shape[1]
    inputs_here = turned.shape[1] // (parities * outputs)
    batch = BATCH
    for first in range(0, group, batch):
        for member in range(first, first + batch):
            for part in range(per_frame):
                window(member, part)
        rows = slice(first * spectra, (first + batch) * spectra)
        near = windowed[rows, : points // 2]
        far = windowed[rows, points // 2 :]
        for parity in range(parities):
            folded = near + far if parity == 0 else near - far
            high = folded.astype(jnp.bfloat16)
            low = (folded - high.astype(jnp.float32)).astype(jnp.bfloat16)
            spectrum = lax.dot_general(
                table_ref[parity],
                jnp.concatenate([high, low, high][:PASSES], axis=1),
                contract,
                preferred_element_type=jnp.float32,
            )
            for member in range(batch):
                start = parity * outputs * inputs_here + step * group + first + member
                for column in range(spectra // LANES):
                    left = member * spectra + column * LANES
                    turned[column, pl.ds(start, outputs, stride=inputs_here), :] = spectrum[
                        :, left : left + LANES
                    ]

    @pl.when(step == pl.num_programs(0) - 1)
    def _():
        chunks = sent.shape[0]
        owners = packed.shape[0] // chunks
        count = outputs * inputs_here // chunks
        copies = []
        for chunk in range(chunks):
            here = slice(chunk * owners, (chunk + 1) * owners)
            for column in range(spectra // LANES):
                columns = slice(column * LANES, (column + 1) * LANES)
                for parity in range(parities):
                    start = (parity * chunks + chunk) * count
                    values = turned[column, start : start + count, :].astype(jnp.bfloat16)
                    packed[here, parity, :, columns] = values.reshape(owners, -1, LANES)
            copies.append(pltpu.make_async_copy(packed.at[here], out_ref.at[here], sent.at[chunk]))
            copies[-1].start()
        for copy in copies:
            copy.wait()


def channelize(samples, filter_taps, owners):
    inputs_here, _, length = samples.shape
    tap_count, points = filter_taps.shape
    frames = length // points
    spectra = frames - tap_count + 1
    halves = points // LANES
    group = 4
    table = fourier_table(points, owners)
    lined = samples.reshape(inputs_here, 2, frames, halves, LANES).transpose(0, 2, 3, 1, 4)
    lined = lined.reshape(-1, LANES)
    rows = lined.shape[0] // inputs_here * group
    shape = (owners, points // owners, 2 * inputs_here, spectra)
    pitch = -(-(spectra // 8 + tap_count - 1) * 2 * halves // 8) * 64
    whole = lambda array: pl.BlockSpec(array.shape, lambda i: (0,) * array.ndim)
    voltage = pl.pallas_call(
        functools.partial(channelize_kernel, frames, spectra, tap_count, group),
        out_shape=jax.ShapeDtypeStruct(shape, jnp.bfloat16),
        grid=(inputs_here // group,),
        in_specs=[
            pl.BlockSpec((rows, LANES), lambda i: (i, 0)),
            whole(filter_taps),
            whole(table),
        ],
        out_specs=pl.BlockSpec(memory_space=pl.ANY),
        scratch_shapes=[
            pltpu.VMEM((group * pitch, LANES), jnp.float32),
            pltpu.VMEM((group * spectra, 2 * points), jnp.float32),
            pltpu.VMEM((spectra // LANES, 2 * points * inputs_here, LANES), jnp.float32),
            pltpu.VMEM(shape, jnp.bfloat16),
            pltpu.SemaphoreType.DMA((4,)),
        ],
        compiler_params=pltpu.CompilerParams(vmem_limit_bytes=60 << 20),
        name="channelize",
    )(lined, filter_taps, jnp.asarray(table))
    return voltage.reshape(owners, points // owners, 2, inputs_here, spectra)


def beam_kernel(scale, volt_ref, weight_ref, out_ref, held, arrived):
    inner, outer, per_device, _, inputs, spectra = volt_ref.shape
    pols, beams = weight_ref.shape[1], weight_ref.shape[-1]
    each = outer // pols
    dishes = each * inner * inputs
    owners, chunk = out_ref.shape[0], out_ref.shape[-1]

    def gathered(channel, pol, part):
        blocks = [
            volt_ref[:, source, channel, part].reshape(inner * inputs, spectra)
            for source in range(pol * each, (pol + 1) * each)
        ]
        return jnp.concatenate(blocks, axis=0).T

    stages = [(channel, pol) for channel in range(per_device) for pol in range(pols)]
    copies = [
        pltpu.make_async_copy(weight_ref.at[stage], held.at[stage], arrived.at[stage]) for stage in stages
    ]
    for copy in copies:
        copy.start()

    def left_side(channel, pol):
        real = gathered(channel, pol, 0)
        imag = gathered(channel, pol, 1)
        return jnp.concatenate(
            [jnp.concatenate([real, -imag], axis=1), jnp.concatenate([imag, real], axis=1)], axis=0
        )

    ready = [left_side(*stage) for stage in stages[:HOIST]]
    for channel in range(per_device):
        total = None
        for pol in range(pols):
            index = channel * pols + pol
            for group in WAITS:
                if group[0] == index:
                    for member in group:
                        copies[member].wait()
            lhs = ready[index] if index < HOIST else left_side(channel, pol)
            weights = held[channel, pol].reshape(2 * dishes, beams)
            formed = jnp.dot(lhs, weights, preferred_element_type=jnp.float32)
            power = formed * formed
            power = power[:spectra] + power[spectra:]
            power = power.reshape(spectra // (8 * INTEG), INTEG, 8, beams).sum(axis=1)
            total = power if total is None else total + power
        total = (total.reshape(spectra // INTEG, beams) * jnp.float32(scale)).astype(jnp.bfloat16)
        for owner in range(owners):
            out_ref[owner, channel] = total[:, owner * chunk : (owner + 1) * chunk]


def beam_power(turned, weights, wide_count):
    per_device, spectra = turned.shape[2], turned.shape[5]
    pols, beams = weights.shape[1], weights.shape[4]
    bins = spectra // INTEG
    vmem = pl.BlockSpec(memory_space=pltpu.VMEM)
    return pl.pallas_call(
        functools.partial(beam_kernel, 1.0 / (pols * INTEG)),
        out_shape=jax.ShapeDtypeStruct((wide_count, per_device, bins, beams // wide_count), jnp.bfloat16),
        in_specs=[vmem, pl.BlockSpec(memory_space=pl.ANY)],
        out_specs=vmem,
        scratch_shapes=[
            pltpu.VMEM(weights.shape, weights.dtype),
            pltpu.SemaphoreType.DMA((per_device, pols)),
        ],
        compiler_params=pltpu.CompilerParams(vmem_limit_bytes=50 << 20),
        name="beam_power",
    )(turned, weights)


def band_kernel(odd_ref, row_ref, out_ref):
    bins, width = row_ref.shape
    block = out_ref.shape[0]
    odd = odd_ref[0] > 0
    for channel in range(block // bins):
        rows = slice(channel * bins, (channel + 1) * bins)
        shifted = pltpu.roll(row_ref[...], channel * bins, axis=1)
        low, high = shifted[:, :block], shifted[:, width - block :]
        out_ref[rows, :block] = shifted[:, block : width - block].astype(jnp.bfloat16)
        out_ref[rows, block : width - block] = jnp.where(odd, low, high).astype(jnp.bfloat16)
        out_ref[rows, width - block :] = jnp.where(odd, high, low).astype(jnp.bfloat16)


def banded(smooth_kernel, odd, channels_here, bins):
    extent = smooth_kernel.shape[0]
    half = extent // 2
    stored = np.arange(bins) // 8 + np.arange(bins) % 8 * (bins // 8)
    distance = stored[None, :] - np.arange(bins)[:, None] + half
    selector = (distance[None] == np.arange(extent)[:, None, None]).astype(ml_dtypes.bfloat16)
    row = jnp.einsum(
        "dtu,kd->tku",
        jnp.asarray(selector),
        smooth_kernel.astype(jnp.bfloat16),
        preferred_element_type=jnp.float32,
    ).reshape(bins, extent * bins)
    width = (channels_here + extent - 1) * bins
    row = jnp.pad(row, ((0, 0), (0, width - extent * bins)))
    vmem = pl.BlockSpec(memory_space=pltpu.VMEM)
    return pl.pallas_call(
        band_kernel,
        out_shape=jax.ShapeDtypeStruct((channels_here * bins, width), jnp.bfloat16),
        in_specs=[pl.BlockSpec(memory_space=pltpu.SMEM), vmem],
        out_specs=vmem,
        compiler_params=pltpu.CompilerParams(vmem_limit_bytes=16 << 20),
        name="band",
    )(odd.astype(jnp.int32).reshape(1), row)


def filtered(refs, matrix):
    centered = []
    for ref in refs:
        channels, bins, beams = ref.shape
        values = ref[...].astype(jnp.float32)
        values = values - jnp.mean(values, axis=1, keepdims=True)
        centered.append(values.astype(jnp.bfloat16).reshape(channels * bins, beams))
    stacked = jnp.concatenate(centered, axis=0)
    return jnp.dot(matrix, stacked, preferred_element_type=jnp.float32)


def near_kernel(mid_ref, matrix_ref, out_ref):
    width = out_ref.shape[0]
    out_ref[...] = filtered((mid_ref,), matrix_ref[:, :width])


def far_kernel(other_ref, pair_ref, part_ref, matrix_ref, out_ref):
    width = part_ref.shape[0]
    result = part_ref[...] + filtered((pair_ref, other_ref), matrix_ref[:, width:])
    out_ref[...] = result.reshape(out_ref.shape)


def smooth(pair, mid, other, matrix):
    channels, bins, beams = mid.shape
    vmem = pl.BlockSpec(memory_space=pltpu.VMEM)
    near = pl.pallas_call(
        near_kernel,
        out_shape=jax.ShapeDtypeStruct((channels * bins, beams), jnp.float32),
        in_specs=[vmem] * 2,
        out_specs=vmem,
        compiler_params=pltpu.CompilerParams(vmem_limit_bytes=16 << 20),
        name="smooth_near",
    )(mid, matrix)
    return pl.pallas_call(
        far_kernel,
        out_shape=jax.ShapeDtypeStruct(mid.shape, jnp.float32),
        in_specs=[vmem] * 4,
        out_specs=vmem,
        compiler_params=pltpu.CompilerParams(vmem_limit_bytes=16 << 20),
        name="smooth_far",
    )(other, pair, near, matrix)


def body(samples, filter_taps, beam_weights, smooth_kernel):
    wide_count = lax.axis_size("wide")
    narrow_count = lax.axis_size("narrow")
    voltage = channelize(samples, filter_taps, wide_count * narrow_count)
    turned = lax.all_to_all(voltage, ("narrow", "wide"), split_axis=0, concat_axis=0, tiled=True)
    turned = turned.reshape(narrow_count, wide_count, *turned.shape[1:])
    per_device, spectra = turned.shape[2], turned.shape[5]
    intensity = beam_power(turned, beam_weights, wide_count)
    intensity, smooth_kernel = lax.optimization_barrier((intensity, smooth_kernel))
    odd = lax.axis_index("narrow") % 2
    matrix = banded(smooth_kernel, odd, per_device * wide_count, spectra // INTEG)
    bins, beams = intensity.shape[2], intensity.shape[3]
    by_beam = lax.all_to_all(intensity, "wide", split_axis=0, concat_axis=0, tiled=True)
    by_beam = by_beam.reshape(-1, bins, beams)
    pairs = [(i, i ^ 1) for i in range(narrow_count)]
    others = [(i, i - 1 + i % 2 * 2) for i in range(1, narrow_count - 1)]
    other = lax.ppermute(by_beam, "narrow", others)
    pair = lax.ppermute(by_beam, "narrow", pairs)
    return smooth(pair, by_beam, other, matrix)


def solution(mesh):
    placed = (
        P(("wide", "narrow"), None, None),
        P(),
        P(("narrow", "wide"), None, None, None, None),
        P(),
    )
    return jax.shard_map(
        body, mesh=mesh, in_specs=placed, out_specs=P("narrow", None, "wide"), check_vma=False
    )
```

```python
import functools

import jax
import jax.numpy as jnp
import ml_dtypes
import numpy as np
from jax import lax
from jax.experimental import pallas as pl
from jax.experimental.pallas import tpu as pltpu
from jax.sharding import PartitionSpec as P

INTEG = 8
HALF = 16
LANES = 128
BATCH = 2
HOIST = 4
WAITS = ((0,), (1, 2, 3))
SHORTEST = 4
PASSES = 3


def fourier_table(points, owners):
    per_device = points // owners
    first = np.arange(owners) * per_device
    channel = first[None, :] + np.arange(per_device)[:, None]
    angle = (channel[:, :, None] * np.arange(points // 2) % points) * (2.0 * np.pi / points)
    cosine = np.cos(angle) / np.sqrt(points)
    sine = np.sin(angle) / np.sqrt(points)
    real_row = np.concatenate([cosine, sine], axis=2)
    imag_row = np.concatenate([-sine, cosine], axis=2)
    table = np.stack([real_row, imag_row], axis=2).reshape(per_device, -1, points)
    table = table.astype(np.float32)
    high = table.astype(ml_dtypes.bfloat16)
    low = (table - high.astype(np.float32)).astype(ml_dtypes.bfloat16)
    return np.concatenate([high, high, low][:PASSES], axis=2)


def fast_filter(taps, value):
    if len(taps) <= SHORTEST:

        def direct(index):
            total = taps[0] * value(index)
            for tap in range(1, len(taps)):
                total = total + taps[tap] * value(index + tap)
            return total

        return direct
    even, odd = taps[0::2], taps[1::2]
    both = [first + second for first, second in zip(even, odd)]
    early = functools.cache(fast_filter(even, lambda index: value(2 * index)))
    late = functools.cache(fast_filter(odd, lambda index: value(2 * index + 1)))
    added = functools.cache(lambda index: value(2 * index + 1) + value(2 * index + 2))
    mixed = functools.cache(fast_filter(both, added))

    def folded(index):
        half = index // 2
        if index % 2 == 0:
            return early(half) + late(half)
        return mixed(half) - (early(half + 1) + late(half))

    return folded


def channelize_kernel(
    frames, spectra, tap_count, group, x_ref, taps_ref, table_ref, out_ref, lined, windowed, turned, packed, sent
):
    step = pl.program_id(0)
    rows = x_ref.shape[0] // group
    per_frame = rows // frames
    segment = spectra // 8
    span = segment * per_frame
    needed = (segment + tap_count - 1) * per_frame
    pitch = lined.shape[0] // group

    for member in range(group):
        for lane in range(8):
            count = min(-(-needed // 8) * 8, rows - lane * span)
            start = member * rows + lane * span
            values = x_ref[start : start + count, :].astype(jnp.float32)
            lined[pl.ds(member * pitch + lane, count, stride=8), :] = values

    def window(member, part):
        half = part // 2
        columns = slice(half * LANES, (half + 1) * LANES)
        taps = [jnp.broadcast_to(taps_ref[t : t + 1, columns], (8, LANES)) for t in range(tap_count)]

        def frame(index):
            start = member * pitch + (per_frame * index + part) * 8
            return lined[start : start + 8, :]

        filtered = fast_filter(taps, frame)
        for index in range(segment):
            row = member * spectra + index * 8
            windowed[row : row + 8, part * LANES : (part + 1) * LANES] = filtered(index)

    contract = (((1,), (1,)), ((), ()))
    parities, outputs, points = table_ref.shape[0], table_ref.shape[1], windowed.shape[1]
    inputs_here = turned.shape[1] // (parities * outputs)
    batch = BATCH
    for first in range(0, group, batch):
        for member in range(first, first + batch):
            for part in range(per_frame):
                window(member, part)
        rows = slice(first * spectra, (first + batch) * spectra)
        near = windowed[rows, : points // 2]
        far = windowed[rows, points // 2 :]
        for parity in range(parities):
            folded = near + far if parity == 0 else near - far
            high = folded.astype(jnp.bfloat16)
            low = (folded - high.astype(jnp.float32)).astype(jnp.bfloat16)
            spectrum = lax.dot_general(
                table_ref[parity],
                jnp.concatenate([high, low, high][:PASSES], axis=1),
                contract,
                preferred_element_type=jnp.float32,
            )
            for member in range(batch):
                start = parity * outputs * inputs_here + step * group + first + member
                for column in range(spectra // LANES):
                    left = member * spectra + column * LANES
                    turned[column, pl.ds(start, outputs, stride=inputs_here), :] = spectrum[
                        :, left : left + LANES
                    ]

    @pl.when(step == pl.num_programs(0) - 1)
    def _():
        chunks = sent.shape[0]
        owners = packed.shape[0] // chunks
        count = outputs * inputs_here // chunks
        copies = []
        for chunk in range(chunks):
            here = slice(chunk * owners, (chunk + 1) * owners)
            for column in range(spectra // LANES):
                columns = slice(column * LANES, (column + 1) * LANES)
                for parity in range(parities):
                    start = (parity * chunks + chunk) * count
                    values = turned[column, start : start + count, :].astype(jnp.bfloat16)
                    packed[here, parity, :, columns] = values.reshape(owners, -1, LANES)
            copies.append(pltpu.make_async_copy(packed.at[here], out_ref.at[here], sent.at[chunk]))
            copies[-1].start()
        for copy in copies:
            copy.wait()


def channelize(samples, filter_taps, owners):
    inputs_here, _, length = samples.shape
    tap_count, points = filter_taps.shape
    frames = length // points
    spectra = frames - tap_count + 1
    halves = points // LANES
    group = 4
    table = fourier_table(points, owners)
    lined = samples.reshape(inputs_here, 2, frames, halves, LANES).transpose(0, 2, 3, 1, 4)
    lined = lined.reshape(-1, LANES)
    rows = lined.shape[0] // inputs_here * group
    shape = (owners, points // owners, 2 * inputs_here, spectra)
    pitch = -(-(spectra // 8 + tap_count - 1) * 2 * halves // 8) * 64
    whole = lambda array: pl.BlockSpec(array.shape, lambda i: (0,) * array.ndim)
    voltage = pl.pallas_call(
        functools.partial(channelize_kernel, frames, spectra, tap_count, group),
        out_shape=jax.ShapeDtypeStruct(shape, jnp.bfloat16),
        grid=(inputs_here // group,),
        in_specs=[
            pl.BlockSpec((rows, LANES), lambda i: (i, 0)),
            whole(filter_taps),
            whole(table),
        ],
        out_specs=pl.BlockSpec(memory_space=pl.ANY),
        scratch_shapes=[
            pltpu.VMEM((group * pitch, LANES), jnp.float32),
            pltpu.VMEM((group * spectra, 2 * points), jnp.float32),
            pltpu.VMEM((spectra // LANES, 2 * points * inputs_here, LANES), jnp.float32),
            pltpu.VMEM(shape, jnp.bfloat16),
            pltpu.SemaphoreType.DMA((8,)),
        ],
        compiler_params=pltpu.CompilerParams(vmem_limit_bytes=60 << 20),
        name="channelize",
    )(lined, filter_taps, jnp.asarray(table))
    return voltage.reshape(owners, points // owners, 2, inputs_here, spectra)


def beam_kernel(scale, volt_ref, weight_ref, out_ref, held, arrived):
    inner, outer, per_device, _, inputs, spectra = volt_ref.shape
    pols, beams = weight_ref.shape[1], weight_ref.shape[-1]
    each = outer // pols
    dishes = each * inner * inputs
    owners, chunk = out_ref.shape[0], out_ref.shape[-1]

    def gathered(channel, pol, part):
        blocks = [
            volt_ref[:, source, channel, part].reshape(inner * inputs, spectra)
            for source in range(pol * each, (pol + 1) * each)
        ]
        return jnp.concatenate(blocks, axis=0).T

    stages = [(channel, pol) for channel in range(per_device) for pol in range(pols)]
    copies = [
        pltpu.make_async_copy(weight_ref.at[stage], held.at[stage], arrived.at[stage]) for stage in stages
    ]
    for copy in copies:
        copy.start()

    def left_side(channel, pol):
        real = gathered(channel, pol, 0)
        imag = gathered(channel, pol, 1)
        return jnp.concatenate(
            [jnp.concatenate([real, -imag], axis=1), jnp.concatenate([imag, real], axis=1)], axis=0
        )

    ready = [left_side(*stage) for stage in stages[:HOIST]]
    for channel in range(per_device):
        total = None
        for pol in range(pols):
            index = channel * pols + pol
            for group in WAITS:
                if group[0] == index:
                    for member in group:
                        copies[member].wait()
            lhs = ready[index] if index < HOIST else left_side(channel, pol)
            weights = held[channel, pol].reshape(2 * dishes, beams)
            formed = jnp.dot(lhs, weights, preferred_element_type=jnp.float32)
            power = formed * formed
            power = power[:spectra] + power[spectra:]
            power = power.reshape(spectra // (8 * INTEG), INTEG, 8, beams).sum(axis=1)
            total = power if total is None else total + power
        total = (total.reshape(spectra // INTEG, beams) * jnp.float32(scale)).astype(jnp.bfloat16)
        for owner in range(owners):
            out_ref[owner, channel] = total[:, owner * chunk : (owner + 1) * chunk]


def beam_power(turned, weights, wide_count):
    per_device, spectra = turned.shape[2], turned.shape[5]
    pols, beams = weights.shape[1], weights.shape[4]
    bins = spectra // INTEG
    vmem = pl.BlockSpec(memory_space=pltpu.VMEM)
    return pl.pallas_call(
        functools.partial(beam_kernel, 1.0 / (pols * INTEG)),
        out_shape=jax.ShapeDtypeStruct((wide_count, per_device, bins, beams // wide_count), jnp.bfloat16),
        in_specs=[vmem, pl.BlockSpec(memory_space=pl.ANY)],
        out_specs=vmem,
        scratch_shapes=[
            pltpu.VMEM(weights.shape, weights.dtype),
            pltpu.SemaphoreType.DMA((per_device, pols)),
        ],
        compiler_params=pltpu.CompilerParams(vmem_limit_bytes=50 << 20),
        name="beam_power",
    )(turned, weights)


def band_kernel(odd_ref, row_ref, out_ref):
    bins, width = row_ref.shape
    block = out_ref.shape[0]
    odd = odd_ref[0] > 0
    for channel in range(block // bins):
        rows = slice(channel * bins, (channel + 1) * bins)
        shifted = pltpu.roll(row_ref[...], channel * bins, axis=1)
        low, high = shifted[:, :block], shifted[:, width - block :]
        out_ref[rows, :block] = shifted[:, block : width - block].astype(jnp.bfloat16)
        out_ref[rows, block : width - block] = jnp.where(odd, low, high).astype(jnp.bfloat16)
        out_ref[rows, width - block :] = jnp.where(odd, high, low).astype(jnp.bfloat16)


def banded(smooth_kernel, odd, channels_here, bins):
    extent = smooth_kernel.shape[0]
    half = extent // 2
    stored = np.arange(bins) // 8 + np.arange(bins) % 8 * (bins // 8)
    distance = stored[None, :] - np.arange(bins)[:, None] + half
    selector = (distance[None] == np.arange(extent)[:, None, None]).astype(ml_dtypes.bfloat16)
    row = jnp.einsum(
        "dtu,kd->tku",
        jnp.asarray(selector),
        smooth_kernel.astype(jnp.bfloat16),
        preferred_element_type=jnp.float32,
    ).reshape(bins, extent * bins)
    width = (channels_here + extent - 1) * bins
    row = jnp.pad(row, ((0, 0), (0, width - extent * bins)))
    vmem = pl.BlockSpec(memory_space=pltpu.VMEM)
    return pl.pallas_call(
        band_kernel,
        out_shape=jax.ShapeDtypeStruct((channels_here * bins, width), jnp.bfloat16),
        in_specs=[pl.BlockSpec(memory_space=pltpu.SMEM), vmem],
        out_specs=vmem,
        compiler_params=pltpu.CompilerParams(vmem_limit_bytes=16 << 20),
        name="band",
    )(odd.astype(jnp.int32).reshape(1), row)


def filtered(refs, matrix):
    centered = []
    for ref in refs:
        channels, bins, beams = ref.shape
        values = ref[...].astype(jnp.float32)
        values = values - jnp.mean(values, axis=1, keepdims=True)
        centered.append(values.astype(jnp.bfloat16).reshape(channels * bins, beams))
    stacked = jnp.concatenate(centered, axis=0)
    return jnp.dot(matrix, stacked, preferred_element_type=jnp.float32)


def near_kernel(mid_ref, matrix_ref, out_ref):
    width = out_ref.shape[0]
    out_ref[...] = filtered((mid_ref,), matrix_ref[:, :width])


def far_kernel(other_ref, pair_ref, part_ref, matrix_ref, out_ref):
    width = part_ref.shape[0]
    result = part_ref[...] + filtered((pair_ref, other_ref), matrix_ref[:, width:])
    out_ref[...] = result.reshape(out_ref.shape)


def smooth(pair, mid, other, matrix):
    channels, bins, beams = mid.shape
    vmem = pl.BlockSpec(memory_space=pltpu.VMEM)
    near = pl.pallas_call(
        near_kernel,
        out_shape=jax.ShapeDtypeStruct((channels * bins, beams), jnp.float32),
        in_specs=[vmem] * 2,
        out_specs=vmem,
        compiler_params=pltpu.CompilerParams(vmem_limit_bytes=16 << 20),
        name="smooth_near",
    )(mid, matrix)
    return pl.pallas_call(
        far_kernel,
        out_shape=jax.ShapeDtypeStruct(mid.shape, jnp.float32),
        in_specs=[vmem] * 4,
        out_specs=vmem,
        compiler_params=pltpu.CompilerParams(vmem_limit_bytes=16 << 20),
        name="smooth_far",
    )(other, pair, near, matrix)


def body(samples, filter_taps, beam_weights, smooth_kernel):
    wide_count = lax.axis_size("wide")
    narrow_count = lax.axis_size("narrow")
    voltage = channelize(samples, filter_taps, wide_count * narrow_count)
    turned = lax.all_to_all(voltage, ("narrow", "wide"), split_axis=0, concat_axis=0, tiled=True)
    turned = turned.reshape(narrow_count, wide_count, *turned.shape[1:])
    per_device, spectra = turned.shape[2], turned.shape[5]
    intensity = beam_power(turned, beam_weights, wide_count)
    intensity, smooth_kernel = lax.optimization_barrier((intensity, smooth_kernel))
    odd = lax.axis_index("narrow") % 2
    matrix = banded(smooth_kernel, odd, per_device * wide_count, spectra // INTEG)
    bins, beams = intensity.shape[2], intensity.shape[3]
    by_beam = lax.all_to_all(intensity, "wide", split_axis=0, concat_axis=0, tiled=True)
    by_beam = by_beam.reshape(-1, bins, beams)
    pairs = [(i, i ^ 1) for i in range(narrow_count)]
    others = [(i, i - 1 + i % 2 * 2) for i in range(1, narrow_count - 1)]
    other = lax.ppermute(by_beam, "narrow", others)
    pair = lax.ppermute(by_beam, "narrow", pairs)
    return smooth(pair, by_beam, other, matrix)


def solution(mesh):
    placed = (
        P(("wide", "narrow"), None, None),
        P(),
        P(("narrow", "wide"), None, None, None, None),
        P(),
    )
    return jax.shard_map(
        body, mesh=mesh, in_specs=placed, out_specs=P("narrow", None, "wide"), check_vma=False
    )
```
